32 devices in a mesh: rows: 2 (over core), tp: 4 (over y, x), attn: 4 (over z).
Axes of the slice: x: 2, y: 2, z: 4, core: 2. Of those that a mesh axis runs over, the one named last changes fastest.
Arguments:
- tokens: bfloat16 [4096, 4096], P(('rows', 'attn')), may hold values from -60 to 60, as said below
- norm_gain: bfloat16 [4096], replicated, may hold values from 0.099609375 to 1.8984375
- w_query: bfloat16 [4096, 2048], P('rows', 'tp'), may hold values from -1 to 1, as said below
- key_projection_weight: bfloat16 [4096, 512], P('rows', 'tp'), may hold values from -8 to 8, as said below
- value_projection_weight: bfloat16 [4096, 512], P('rows', 'tp'), may hold values from -0.09375 to 0.09375
- documents: int32 [2, 2048], P('rows'), may hold values from 0 to 5, never falling along the last dimension, each value on 1 to 1024 neighbouring positions
Outputs:
- attn_out: bfloat16 [4096, 2048], P(('rows', 'attn'), 'tp')
The draws below stay inside these ranges and needn't reach their ends.
Inputs may be any that keep to these rules, and one draw needn't show every extreme that they name: `tokens`: activations of order one. `w_query`: entries of order 4096 ** -0.5. `key_projection_weight`: entries of order one or smaller. `documents`: along each window the document numbers never fall; every document spans 1 to 1024 tokens and some document of each window spans exactly 1024.
All inputs are finite; a program needn't handle non-finite values.
Results may differ from the reference program's by a relative error of at most 0.012.
The reference program's roundings to bfloat16 on the way count: a program that leaves them out, or rounds other values in their place, can miss the bound.
Values may be sent and summed in bfloat16 or wider, within the bound.
A program may use at most 64 MiB of HBM per device.

```python
import math
import jax
import jax.numpy as jnp
import numpy as np
from jax import lax

MODEL_WIDTH = 4096
QUERY_HEADS = 16
KEY_VALUE_HEADS = 4
HEAD_SIZE = 128
DOCS = 6
WINDOW_TOKENS = 2048
MOST = 1024
TOKENS = 4096
N_ROWS = 2


def draw_tokens(key, part):
    base = jax.random.normal(jax.random.fold_in(key, 11), (TOKENS, MODEL_WIDTH), jnp.float32)
    row_scale = jnp.exp(jax.random.uniform(jax.random.fold_in(key, 12), (TOKENS, 1), jnp.float32, math.log(0.3), math.log(3.0)))
    column_scale = jnp.exp(jax.random.uniform(jax.random.fold_in(key, 13), (1, MODEL_WIDTH), jnp.float32, math.log(0.3), math.log(3.0)))
    return jnp.clip(base * row_scale * column_scale, -60.0, 60.0).astype(jnp.bfloat16)


def projection_pair(key):
    query_matrix = jax.random.normal(jax.random.fold_in(key, 21), (MODEL_WIDTH, QUERY_HEADS * HEAD_SIZE), jnp.float32) * MODEL_WIDTH ** (-0.5)
    key_matrix = jax.random.normal(jax.random.fold_in(key, 22), (MODEL_WIDTH, KEY_VALUE_HEADS * HEAD_SIZE), jnp.float32) * MODEL_WIDTH ** (-0.5)
    return (jnp.clip(query_matrix, -1.0, 1.0), jnp.clip(key_matrix, -8.0, 8.0))


def draw_w_query(key, part):
    return projection_pair(key)[0].astype(jnp.bfloat16)


def draw_key_projection_weight(key, part):
    return projection_pair(key)[1].astype(jnp.bfloat16)


def block_scale(stream_key, extent, shards, smallest, high):
    level = 1.0
    for axis_at, blocks in shards:
        draws = jax.random.uniform(jax.random.fold_in(jax.random.fold_in(stream_key, 6), axis_at), (blocks,), jnp.float32, smallest / len(shards), high / len(shards))
        level = level * jnp.repeat(jnp.exp(draws), extent[axis_at] // blocks).reshape((-1,) + (1,) * (len(extent) - 1 - axis_at))
    return level


def length_profile(amount, total, limit, skew):
    loads = [(1 << 20) // math.isqrt(standing ** skew) + 1 for standing in range(2, amount + 1)]
    spare, given = total - limit - (amount - 1), [1] * (amount - 1)
    while spare > 0:
        movable = [i for i in range(amount - 1) if given[i] < limit]
        mass, left = sum([loads[i] for i in movable]), spare
        for i in movable:
            more = min(limit - given[i], max(1, left * loads[i] // mass), spare)
            given[i] = given[i] + more
            spare = spare - more
    return np.array([limit] + given)


def ragged_sizes(stream_key, count, total, most, lean):
    if count == 2:
        one = jax.random.randint(stream_key, (), max(1, total - most), min(most, total - 1) + 1)
        return jnp.stack([one, total - one])
    lengths = jnp.asarray(length_profile(count, total, most, lean), jnp.int32)
    pairs = (count - 1) // 2
    source_of, receiver = lengths[1:1 + 2 * pairs:2], lengths[2:2 + 2 * pairs:2]
    margin = jnp.minimum(source_of - 1, most - receiver)
    shifted = jax.random.randint(jax.random.fold_in(stream_key, 1), (pairs,), 0, 1 << 20) % (margin + 1)
    lengths = lengths.at[1:1 + 2 * pairs:2].set(source_of - shifted).at[2:2 + 2 * pairs:2].set(receiver + shifted)
    return lengths[jax.random.permutation(jax.random.fold_in(stream_key, 2), count)]


def gaussian(own_key, shape, scale, limit, pieces=(), kind=jnp.bfloat16):
    result = jax.random.normal(own_key, shape, jnp.float32) * scale
    if len(pieces) > 0:
        result = block_scale(own_key, shape, pieces, -0.22, 0.18) * result
    return jnp.clip(result, min=-limit, max=limit).astype(kind)


def setup_inputs(seed: int = 0) -> dict:
    streams_of = jax.random.split(jax.random.key(seed), 7)
    tokens = draw_tokens(jax.random.fold_in(streams_of[6], 71), 0)
    norm_gain = jnp.clip(1.0 + 0.18 * jax.random.normal(streams_of[1], (MODEL_WIDTH,), jnp.float32), 0.099609375, 1.8984375).astype(jnp.bfloat16)
    w_query = draw_w_query(jax.random.fold_in(streams_of[6], 71), 0)
    key_projection_weight = draw_key_projection_weight(jax.random.fold_in(streams_of[6], 71), 0)
    value_projection_weight = gaussian(streams_of[4], (MODEL_WIDTH, KEY_VALUE_HEADS * HEAD_SIZE), MODEL_WIDTH ** -0.5, 0.09375, ((0, 2), (1, 4)))
    documents = jax.vmap(lambda own: jnp.searchsorted(jnp.cumsum(ragged_sizes(own, DOCS, WINDOW_TOKENS, MOST, 2)), jnp.arange(WINDOW_TOKENS), side="right"))(jax.random.split(streams_of[5], N_ROWS)).reshape((N_ROWS, WINDOW_TOKENS)).astype(jnp.int32)
    return {"tokens": tokens, "norm_gain": norm_gain, "w_query": w_query, "key_projection_weight": key_projection_weight, "value_projection_weight": value_projection_weight, "documents": documents}


def rotary(vectors, positions):
    head_dim = vectors.shape[-1]
    half_dim = head_dim // 2
    frequency = jnp.exp(jnp.arange(half_dim, dtype=jnp.float32) * (-2.0 * math.log(500000.0) / head_dim))
    angles = positions.astype(jnp.float32)[:, None] * frequency[None, :]
    cosine_table = jnp.cos(angles)[:, None, :]
    sine_table = jnp.sin(angles)[:, None, :]
    first_half = vectors[..., :half_dim]
    second_half = vectors[..., half_dim:]
    return jnp.concatenate([first_half * cosine_table - second_half * sine_table, second_half * cosine_table + first_half * sine_table], axis=-1)

def rms_normed(tokens, norm_gain):
    widened = tokens.astype(jnp.float32)
    mean_sq = lax.optimization_barrier(jnp.mean(widened * widened, axis=-1, keepdims=True))
    return (widened * lax.rsqrt(mean_sq + 1e-05) * norm_gain.astype(jnp.float32)).astype(jnp.bfloat16)

def reference(tokens, norm_gain, w_query, key_projection_weight, value_projection_weight, documents):
    group_width = QUERY_HEADS // KEY_VALUE_HEADS
    score_scale = 1.0 / math.sqrt(HEAD_SIZE)
    windows = tokens.reshape(N_ROWS, WINDOW_TOKENS, MODEL_WIDTH)

    def one_window(inputs):
        window, doc_ids = inputs
        normalized_input = rms_normed(window, norm_gain)
        positions = jnp.arange(WINDOW_TOKENS, dtype=jnp.int32)
        query_proj = jnp.dot(normalized_input, w_query, preferred_element_type=jnp.float32).reshape(WINDOW_TOKENS, QUERY_HEADS, HEAD_SIZE)
        key_projected = jnp.dot(normalized_input, key_projection_weight, preferred_element_type=jnp.float32).reshape(WINDOW_TOKENS, KEY_VALUE_HEADS, HEAD_SIZE)
        query_vectors_all = rotary(query_proj, positions).astype(jnp.bfloat16)
        keys_all = rotary(key_projected, positions).astype(jnp.bfloat16)
        value_vectors_all = jnp.dot(normalized_input, value_projection_weight, preferred_element_type=jnp.float32).astype(jnp.bfloat16).reshape(WINDOW_TOKENS, KEY_VALUE_HEADS, HEAD_SIZE)
        visible = (doc_ids[:, None] == doc_ids[None, :]) & (positions[:, None] >= positions[None, :])
        grouped_heads = query_vectors_all.reshape(WINDOW_TOKENS, KEY_VALUE_HEADS, group_width, HEAD_SIZE)

        def single_head(head_index):
            query_head = lax.dynamic_index_in_dim(grouped_heads, head_index, 1, keepdims=False)
            key_head = lax.dynamic_index_in_dim(keys_all, head_index, 1, keepdims=False)
            value_head = lax.dynamic_index_in_dim(value_vectors_all, head_index, 1, keepdims=False)
            scores = jnp.einsum('pgd,jd->gpj', query_head.astype(jnp.float32), key_head.astype(jnp.float32)) * score_scale
            scores = jnp.where(visible[None], scores, -1e+30)
            row_max = lax.optimization_barrier(jnp.max(scores, axis=-1, keepdims=True))
            weights = jnp.where(visible[None], jnp.exp(scores - row_max), 0.0)
            row_total = lax.optimization_barrier(jnp.sum(weights, axis=-1))
            rounded = weights.astype(jnp.bfloat16)
            mixed_out = jnp.einsum('gpj,jd->gpd', rounded.astype(jnp.float32), value_head.astype(jnp.float32))
            return mixed_out / row_total[..., None]
        split_by_head = lax.map(single_head, jnp.arange(KEY_VALUE_HEADS, dtype=jnp.int32))
        return jnp.transpose(split_by_head, (2, 0, 1, 3)).reshape(WINDOW_TOKENS, QUERY_HEADS * HEAD_SIZE).astype(jnp.bfloat16)
    outputs = lax.map(one_window, (windows, documents))
    return outputs.reshape(N_ROWS * WINDOW_TOKENS, QUERY_HEADS * HEAD_SIZE)
```

```python
import functools
import math

import jax
import jax.numpy as jnp
import numpy as np
from jax import lax
from jax.experimental import pallas as pl
from jax.experimental.pallas import tpu as pltpu
from jax.sharding import PartitionSpec as P

HEAD = 128
MOST = 1024
TQ = 128
BF16 = jnp.bfloat16
F32 = jnp.float32
MESH = pl.DeviceIdType.MESH


def rotary_table(window):
    half = HEAD // 2
    frequency = np.exp(
        np.arange(half, dtype=np.float32) * np.float32(-2.0 * math.log(500000.0) / HEAD)
    ).astype(np.float32)
    angles = np.arange(window, dtype=np.float32)[:, None] * frequency[None, :]
    return np.concatenate([np.cos(angles), np.sin(angles)], axis=1).astype(np.float32)


def kernel(
    n_rows, n_attn, back, chunk,
    tok, gain, wq, wk, wv, docs, table, out,
    gains, xt, xn, wkv_buf, wq_buf, kv, q, tab, kdoc, qdoc,
    tok_sem, own_sem, w_send, w_recv, kv_send, kv_recv,
):
    rows = tok.shape[0]
    depth = wk.shape[0]
    kvw = wk.shape[1]
    qw = wq.shape[1]
    kv_heads = kvw // HEAD
    group = qw // kvw
    chunks = rows // chunk
    tiles = rows // TQ
    mine = back * rows
    span = min(mine + rows, -(-(MOST - 1 + TQ) // TQ) * TQ)
    me = lax.axis_index("rows")
    at = lax.axis_index("attn")

    tok_copies = [
        pltpu.make_async_copy(
            tok.at[pl.ds(c * chunk, chunk)], xt.at[pl.ds(c * chunk, chunk)], tok_sem.at[c]
        )
        for c in range(chunks)
    ]
    own_copies = [
        pltpu.make_async_copy(wk, wkv_buf.at[0, :, pl.ds(0, kvw)], own_sem.at[0]),
        pltpu.make_async_copy(wv, wkv_buf.at[0, :, pl.ds(kvw, kvw)], own_sem.at[1]),
        pltpu.make_async_copy(wq, wq_buf.at[0], own_sem.at[2]),
        pltpu.make_async_copy(
            table.at[pl.ds(pl.multiple_of(at * rows, rows), rows)], tab, own_sem.at[3]
        ),
    ]
    tok_copies[-1].start()
    own_copies[0].start()
    own_copies[1].start()
    own_copies[3].start()
    for copy in tok_copies[-2::-1]:
        copy.start()

    barrier = pltpu.get_barrier_semaphore()
    for d in range(1, n_rows):
        pl.semaphore_signal(
            barrier, inc=1, device_id={"rows": lax.rem(me + d, n_rows)}, device_id_type=MESH
        )
    has_prev = at > 0
    has_next = at < n_attn - 1
    if back:

        @pl.when(has_prev)
        def _():
            pl.semaphore_signal(
                barrier, inc=1, device_id={"attn": at - 1}, device_id_type=MESH
            )

        @pl.when(has_next)
        def _():
            pl.semaphore_signal(
                barrier, inc=1, device_id={"attn": at + 1}, device_id_type=MESH
            )

        pl.semaphore_wait(
            barrier, n_rows - 1 + has_prev.astype(jnp.int32) + has_next.astype(jnp.int32)
        )
    elif n_rows > 1:
        pl.semaphore_wait(barrier, n_rows - 1)

    def weight_copy(d, which):
        src, dst = (
            (wk, wkv_buf.at[d, :, pl.ds(0, kvw)]),
            (wv, wkv_buf.at[d, :, pl.ds(kvw, kvw)]),
            (wq, wq_buf.at[d]),
        )[which]
        return pltpu.make_async_remote_copy(
            src_ref=src, dst_ref=dst,
            send_sem=w_send.at[d, which], recv_sem=w_recv.at[d, which],
            device_id={"rows": lax.rem(me + d, n_rows)}, device_id_type=MESH,
        )

    for which in range(3):
        for d in range(1, n_rows):
            weight_copy(d, which).start()
    own_copies[2].start()

    for s in range(back + 1):
        block = at - back + s
        keep = pl.multiple_of(jnp.maximum(block, 0) * rows, rows)
        kdoc[:, pl.ds(s * rows, rows)] = jnp.where(block >= 0, docs[:, pl.ds(keep, rows)], -1)
    for t in range(tiles):
        row = kdoc[:, pl.ds(mine + t * TQ, TQ)]
        qdoc[pl.ds(t * TQ, TQ), :] = jnp.broadcast_to(row, (TQ, TQ)).T
    for s in range(back):

        @pl.when(at - back + s < 0)
        def _():
            kv[pl.ds(s * rows, rows), :] = jnp.zeros((rows, 2 * kvw), BF16)

    lane = lax.broadcasted_iota(jnp.int32, (1, HEAD), 1)

    def tables(start, size):
        t = tab[pl.ds(start, size), :]
        swapped = pltpu.roll(t, HEAD // 2, 1)
        low = lane < HEAD // 2
        return jnp.where(low, t, swapped), jnp.where(low, -swapped, t)

    def rotate(u, cosine, sine):
        return (u * cosine + pltpu.roll(u, HEAD // 2, 1) * sine).astype(BF16)

    def project(start, size, weights):
        total = None
        for d in range(n_rows):
            owner = lax.rem(me - d + n_rows, n_rows)
            part = jnp.dot(
                xn[pl.ds(start, size), pl.ds(pl.multiple_of(owner * depth, depth), depth)],
                weights[d],
                preferred_element_type=F32,
            )
            total = part if total is None else total + part
        return total

    def hop(s, c):
        return pltpu.make_async_remote_copy(
            src_ref=kv.at[pl.ds((back - s) * rows + c * chunk, chunk)],
            dst_ref=kv.at[pl.ds((back - s - 1) * rows + c * chunk, chunk)],
            send_sem=kv_send.at[s, c], recv_sem=kv_recv.at[s, c],
            device_id={"attn": jnp.minimum(at + 1, n_attn - 1)}, device_id_type=MESH,
        )

    def arrived(s, c):
        @pl.when(at > s)
        def _():
            hop(s, c).wait_recv()

        if s + 1 < back:

            @pl.when((at > s) & has_next)
            def _():
                hop(s + 1, c).start()

    relayed = [(s, c) for s in range(back - 1) for c in reversed(range(chunks))]
    strip, piece = 16, 256
    width = tok.shape[1]
    gains[...] = jnp.broadcast_to(gain[...].astype(F32).reshape(1, -1), gains.shape)
    for c in reversed(range(chunks)):
        if c == 0 and relayed:
            arrived(*relayed.pop(0))
        tok_copies[c].wait()

        @pl.loop(0, chunk // strip, unroll=4)
        def _(i):
            here = pl.ds(pl.multiple_of(c * chunk + i * strip, strip), strip)
            squares = jnp.zeros((strip, piece), F32)
            for k in range(width // piece):
                x = xt[here, pl.ds(k * piece, piece)].astype(F32)
                squares = squares + x * x
            mean_sq = jnp.sum(squares, axis=-1, keepdims=True) * (1.0 / width)
            scale = jnp.broadcast_to(lax.rsqrt(mean_sq + 1e-05), (strip, piece))
            for k in range(width // piece):
                cols = pl.ds(k * piece, piece)
                x = xt[here, cols].astype(F32) * scale
                xn[here, cols] = (
                    x.reshape(strip // 8, 8, piece) * gains[:, cols][None]
                ).reshape(strip, piece).astype(BF16)

        if c == chunks - 1:
            own_copies[0].wait()
            own_copies[1].wait()
            own_copies[3].wait()
            for d in range(1, n_rows):
                weight_copy(d, 0).wait()
                weight_copy(d, 1).wait()
        total = project(c * chunk, chunk, wkv_buf)
        cosine, sine = tables(c * chunk, chunk)
        here = pl.ds(mine + c * chunk, chunk)
        for h in range(kv_heads):
            kv[here, pl.ds(h * HEAD, HEAD)] = rotate(
                total[:, h * HEAD : (h + 1) * HEAD], cosine, sine
            )
        kv[here, pl.ds(kvw, kvw)] = total[:, kvw:].astype(BF16)
        if back:

            @pl.when(has_next)
            def _():
                hop(0, c).start()

    last = [(back - 1, c) for c in reversed(range(chunks))] if back else []

    own_copies[2].wait()
    for d in range(1, n_rows):
        weight_copy(d, 2).wait()
    part = min(rows, 2 * chunk)
    for step in reversed(range(rows // part)):
        for _ in range(min(1, len(relayed))):
            arrived(*relayed.pop(0))
        total = project(step * part, part, wq_buf)
        cosine, sine = tables(step * part, part)
        for h in range(kv_heads):
            for g in range(group):
                col = (h * group + g) * HEAD
                u = rotate(total[:, col : col + HEAD], cosine, sine)
                for t in range(part // TQ):
                    q[step * (part // TQ) + t, h, pl.ds(g * TQ, TQ), :] = u[
                        t * TQ : (t + 1) * TQ
                    ]
    for event in relayed:
        arrived(*event)

    factor = math.log2(math.e) / math.sqrt(HEAD)

    for t in reversed(range(tiles)):
        first = t * TQ
        begin = max(mine + first + TQ - span, 0)
        while last and (last[0][1] + 1) * chunk > begin:
            arrived(*last.pop(0))
        query_at = lax.broadcasted_iota(jnp.int32, (TQ, 1), 0) + (mine + first)
        key_at = lax.broadcasted_iota(jnp.int32, (1, span), 1) + begin
        visible = (qdoc[pl.ds(first, TQ), :][:, :1] == kdoc[:, pl.ds(begin, span)]) & (
            query_at >= key_at
        )
        for h in range(kv_heads):
            keys = kv[pl.ds(begin, span), pl.ds(h * HEAD, HEAD)]
            vals = kv[pl.ds(begin, span), pl.ds(kvw + h * HEAD, HEAD)]
            s = lax.dot_general(
                q[t, h], keys, (((1,), (1,)), ((), ())), preferred_element_type=F32
            )
            s = jnp.where(visible[None], s.reshape(group, TQ, span), -1e30)
            p = jnp.exp2((s - jnp.max(s, axis=-1, keepdims=True)) * factor)
            total = jnp.sum(p, axis=-1, keepdims=True)
            mixed = jnp.dot(
                p.astype(BF16).reshape(group * TQ, span), vals, preferred_element_type=F32
            )
            mixed = (mixed.reshape(group, TQ, HEAD) / total).astype(BF16)
            for g in range(group):
                out[pl.ds(first, TQ), pl.ds((h * group + g) * HEAD, HEAD)] = mixed[g]
    for event in last:
        arrived(*event)

    for s in range(back):
        for c in range(chunks):

            @pl.when((at >= s) & has_next)
            def _():
                hop(s, c).wait_send()


def solution(mesh):
    n_rows = mesh.shape["rows"]
    n_attn = mesh.shape["attn"]

    def on_device(tokens, norm_gain, w_query, w_key, w_value, documents):
        rows, width = tokens.shape
        depth, qw = w_query.shape
        kvw = w_key.shape[1]
        back = min(n_attn - 1, -(-(MOST - 1) // rows))
        chunk = min(rows, TQ)
        chunks = rows // chunk
        table = jnp.asarray(rotary_table(documents.shape[1]))
        anywhere = pl.BlockSpec(memory_space=pl.ANY)
        vmem = pl.BlockSpec(memory_space=pltpu.VMEM)
        keys = (back + 1) * rows
        group = qw // kvw
        return pl.pallas_call(
            functools.partial(kernel, n_rows, n_attn, back, chunk),
            out_shape=pltpu.VMEM((rows, qw), BF16),
            in_specs=[anywhere, vmem, anywhere, anywhere, anywhere, vmem, anywhere],
            out_specs=vmem,
            scratch_shapes=[
                pltpu.VMEM((8, width), F32),
                pltpu.VMEM((rows, width), BF16),
                pltpu.VMEM((rows, width), BF16),
                pltpu.VMEM((n_rows, depth, 2 * kvw), BF16),
                pltpu.VMEM((n_rows, depth, qw), BF16),
                pltpu.VMEM((keys, 2 * kvw), BF16),
                pltpu.VMEM((rows // TQ, kvw // HEAD, group * TQ, HEAD), BF16),
                pltpu.VMEM((rows, HEAD), F32),
                pltpu.VMEM((1, keys), jnp.int32),
                pltpu.VMEM((rows, TQ), jnp.int32),
                pltpu.SemaphoreType.DMA((chunks,)),
                pltpu.SemaphoreType.DMA((4,)),
                pltpu.SemaphoreType.DMA((n_rows, 3)),
                pltpu.SemaphoreType.DMA((n_rows, 3)),
                pltpu.SemaphoreType.DMA((max(back, 1), chunks)),
                pltpu.SemaphoreType.DMA((max(back, 1), chunks)),
            ],
            compiler_params=pltpu.CompilerParams(
                collective_id=0, has_side_effects=True, vmem_limit_bytes=40 << 20
            ),
            name="layer",
        )(*(pltpu.with_memory_space_constraint(a, pltpu.HBM) for a in (tokens, norm_gain, w_query, w_key, w_value, documents, table)))

    placed = (
        P(("rows", "attn"), None),
        P(),
        P("rows", "tp"),
        P("rows", "tp"),
        P("rows", "tp"),
        P("rows", None),
    )
    return jax.shard_map(
        on_device, mesh=mesh, in_specs=placed, out_specs=P(("rows", "attn"), "tp"), check_vma=False
    )
```

```python
import functools
import math

import jax
import jax.numpy as jnp
import numpy as np
from jax import lax
from jax.experimental import pallas as pl
from jax.experimental.pallas import tpu as pltpu
from jax.sharding import PartitionSpec as P

HEAD = 128
MOST = 1024
TQ = 128
BF16 = jnp.bfloat16
F32 = jnp.float32
MESH = pl.DeviceIdType.MESH


def rotary_table(window):
    half = HEAD // 2
    frequency = np.exp(
        np.arange(half, dtype=np.float32) * np.float32(-2.0 * math.log(500000.0) / HEAD)
    ).astype(np.float32)
    angles = np.arange(window, dtype=np.float32)[:, None] * frequency[None, :]
    return np.concatenate([np.cos(angles), np.sin(angles)], axis=1).astype(np.float32)


def kernel(
    n_rows, n_attn, back, block, part,
    tok, gain, wq, wk, wv, docs, table, out,
    gains, xt, xn, wkv_buf, wq_buf, kbuf, vbuf, q, tops, acc, tab, kdoc, qdoc,
    tok_sem, own_sem, w_send, w_recv, kv_send, kv_recv, ready,
):
    rows, width = tok.shape
    depth, kvw = wk.shape
    qw = wq.shape[1]
    kv_heads = kvw // HEAD
    group = qw // kvw
    parts = qw // part
    tiles = rows // TQ
    mine = back * rows
    span = min(mine + rows, -(-(MOST - 1 + TQ) // TQ) * TQ)
    me = lax.axis_index("rows")
    at = lax.axis_index("attn")
    has_prev = at > 0
    has_next = at < n_attn - 1

    def tok_copy(c):
        here = pl.ds(c * TQ, TQ)
        return pltpu.make_async_copy(tok.at[here], xt.at[here], tok_sem.at[c])

    weights = [
        (wk, lambda d: wkv_buf.at[d, :, pl.ds(0, kvw)]),
        (wv, lambda d: wkv_buf.at[d, :, pl.ds(kvw, kvw)]),
    ] + [
        (wq.at[:, pl.ds(j * part, part)], lambda d, j=j: wq_buf.at[j, d]) for j in range(parts)
    ]

    def own_copy(i):
        src, dst = weights[i]
        return pltpu.make_async_copy(src, dst(0), own_sem.at[i])

    def weight_copy(d, i):
        src, dst = weights[i]
        return pltpu.make_async_remote_copy(
            src_ref=src, dst_ref=dst(d),
            send_sem=w_send.at[d, i], recv_sem=w_recv.at[d, i],
            device_id={"rows": lax.rem(me + d, n_rows)}, device_id_type=MESH,
        )

    tab_copy = pltpu.make_async_copy(
        table.at[pl.ds(pl.multiple_of(at * rows, rows), rows)], tab, own_sem.at[len(weights)]
    )

    tok_copy(tiles - 1).start()
    own_copy(0).start()
    for c in reversed(range(tiles - 1)):
        tok_copy(c).start()
        if c == tiles - 2:
            tab_copy.start()
            own_copy(1).start()

    barrier = pltpu.get_barrier_semaphore()
    paired = n_rows == 2 and n_attn > 1
    if paired:
        first = me == 0

        @pl.when(jnp.logical_not(first))
        def _():
            pl.semaphore_signal(barrier, inc=1, device_id={"rows": 0}, device_id_type=MESH)

        @pl.when(first)
        def _():
            pl.semaphore_wait(barrier, 1)
            pl.semaphore_signal(ready, inc=1, device_id={"rows": 1}, device_id_type=MESH)

        @pl.when(jnp.logical_not(first))
        def _():
            pl.semaphore_wait(ready, 1)
    else:
        for d in range(1, n_rows):
            pl.semaphore_signal(
                barrier, inc=1, device_id={"rows": lax.rem(me + d, n_rows)}, device_id_type=MESH
            )
        if back:

            @pl.when(has_prev)
            def _():
                pl.semaphore_signal(
                    barrier, inc=1, device_id={"attn": at - 1}, device_id_type=MESH
                )

            pl.semaphore_wait(barrier, n_rows - 1 + has_next.astype(jnp.int32))
        elif n_rows > 1:
            pl.semaphore_wait(barrier, n_rows - 1)

    for i in range(len(weights)):
        for d in range(1, n_rows):
            weight_copy(d, i).start()
    if paired:

        @pl.when(has_prev)
        def _():
            pl.semaphore_signal(
                barrier, inc=1, device_id={"rows": 1, "attn": at - 1}, device_id_type=MESH
            )

    for i in range(2, len(weights)):
        own_copy(i).start()

    for s in range(back + 1):
        owner = at - back + s
        keep = pl.multiple_of(jnp.maximum(owner, 0) * rows, rows)
        kdoc[:, pl.ds(s * rows, rows)] = jnp.where(owner >= 0, docs[:, pl.ds(keep, rows)], -1)
    for t in range(tiles):
        row = kdoc[:, pl.ds(mine + t * TQ, TQ)]
        qdoc[pl.ds(t * TQ, TQ), :] = jnp.broadcast_to(row, (TQ, TQ)).T
    for s in range(back):

        @pl.when(at - back + s < 0)
        def _():
            kbuf[pl.ds(s * rows, rows), :] = jnp.zeros((rows, kvw), BF16)
            vbuf[pl.ds(s * rows, rows), :] = jnp.zeros((rows, kvw), BF16)

    gains[...] = jnp.broadcast_to(gain[...].astype(F32).reshape(1, -1), gains.shape)

    pieces = [(which, rows - block, block) for which in range(2)]
    for c in reversed(range((rows - block) // TQ)):
        pieces += [(which, c * TQ, TQ) for which in range(2)]

    def hop(s, p):
        which, start, size = pieces[p]
        ref = (kbuf, vbuf)[which]
        return pltpu.make_async_remote_copy(
            src_ref=ref.at[pl.ds((back - s) * rows + start, size)],
            dst_ref=ref.at[pl.ds((back - s - 1) * rows + start, size)],
            send_sem=kv_send.at[s, p], recv_sem=kv_recv.at[s, p],
            device_id={"attn": jnp.minimum(at + 1, n_attn - 1)}, device_id_type=MESH,
        )

    def send(wanted):
        if back:

            @pl.when(has_next)
            def _():
                for p in wanted:
                    hop(0, p).start()

    def arrived(s, p):
        @pl.when(at > s)
        def _():
            hop(s, p).wait_recv()

        if s + 1 < back:

            @pl.when((at > s) & has_next)
            def _():
                hop(s + 1, p).start()

    relays = [(s, p) for s in range(back - 1) for p in range(len(pieces))]
    last = [(back - 1, p) for p in range(len(pieces))] if back else []

    def relay(count):
        for _ in range(min(count, len(relays))):
            arrived(*relays.pop(0))

    strip, piece = 16, 256

    def norm(c):
        tok_copy(c).wait()

        @pl.loop(0, TQ // strip, unroll=4)
        def _(i):
            here = pl.ds(pl.multiple_of(c * TQ + i * strip, strip), strip)
            squares = jnp.zeros((strip, piece), F32)
            for k in range(width // piece):
                x = xt[here, pl.ds(k * piece, piece)].astype(F32)
                squares = squares + x * x
            mean_sq = jnp.sum(squares, axis=-1, keepdims=True) * (1.0 / width)
            scale = jnp.broadcast_to(lax.rsqrt(mean_sq + 1e-05), (strip, piece))
            for k in range(width // piece):
                cols = pl.ds(k * piece, piece)
                x = xt[here, cols].astype(F32) * scale
                xn[here, cols] = (
                    x.reshape(strip // 8, 8, piece) * gains[:, cols][None]
                ).reshape(strip, piece).astype(BF16)

    lane = lax.broadcasted_iota(jnp.int32, (1, HEAD), 1)

    def tables(start, size):
        t = tab[pl.ds(start, size), :]
        swapped = pltpu.roll(t, HEAD // 2, 1)
        low = lane < HEAD // 2
        return jnp.where(low, t, swapped), jnp.where(low, -swapped, t)

    def rotate(u, cosine, sine):
        return (u * cosine + pltpu.roll(u, HEAD // 2, 1) * sine).astype(BF16)

    def term(d, start, size, weight):
        owner = lax.rem(me - d + n_rows, n_rows)
        return jnp.dot(
            xn[pl.ds(start, size), pl.ds(pl.multiple_of(owner * depth, depth), depth)],
            weight,
            preferred_element_type=F32,
        )

    def project(start, size, weight_of, before=lambda d: None):
        before(0)
        total = term(0, start, size, weight_of(0))
        for d in range(1, n_rows):
            before(d)
            total = total + term(d, start, size, weight_of(d))
        return total

    def ready_weight(i):
        def wait(d):
            if d == 0:
                own_copy(i).wait()
            else:
                weight_copy(d, i).wait_recv()

        return wait

    def store_keys(start, size, total):
        cosine, sine = tables(start, size)
        for h in range(kv_heads):
            cols = pl.ds(h * HEAD, HEAD)
            kbuf[pl.ds(mine + start, size), cols] = rotate(
                total[:, h * HEAD : (h + 1) * HEAD], cosine, sine
            )

    def store_values(start, size, total):
        vbuf[pl.ds(mine + start, size), :] = total.astype(BF16)

    high = rows - block
    for c in reversed(range(high // TQ, tiles)):
        norm(c)
    tab_copy.wait()
    total = project(high, block, lambda d: wkv_buf[d, :, pl.ds(0, kvw)], ready_weight(0))
    if paired:

        @pl.when(has_next & jnp.logical_not(first))
        def _():
            pl.semaphore_wait(barrier, 2)
            pl.semaphore_signal(ready, inc=1, device_id={"rows": 0}, device_id_type=MESH)

    store_keys(high, block, total)
    if paired:

        @pl.when(has_next & first)
        def _():
            pl.semaphore_wait(ready, 1)

    send([0])
    total = project(high, block, lambda d: wkv_buf[d, :, pl.ds(kvw, kvw)], ready_weight(1))
    store_values(high, block, total)
    send([1])
    sent = 2
    for b in reversed(range(high // block)):
        for c in reversed(range(block // TQ)):
            norm(b * (block // TQ) + c)
        total = project(b * block, block, lambda d: wkv_buf[d])
        store_keys(b * block, block, total[:, :kvw])
        store_values(b * block, block, total[:, kvw:])
        count = 2 * (block // TQ)
        send(range(sent, sent + count))
        sent += count

    for j in range(parts):
        total = project(0, rows, lambda d: wq_buf[j, d], ready_weight(2 + j))
        cosine, sine = tables(0, rows)
        for k in range(part // HEAD):
            h, g = divmod(j * (part // HEAD) + k, group)
            u = rotate(total[:, k * HEAD : (k + 1) * HEAD], cosine, sine)
            for t in range(tiles):
                q[t, h, pl.ds(g * TQ, TQ), :] = u[t * TQ : (t + 1) * TQ]
        relay(1)

    factor = math.log2(math.e) / math.sqrt(HEAD)

    def attend(t, s, lo, size, opens, closes):
        seen = s * rows + lo
        keys_at = pl.ds(seen, size)
        visible = jnp.tile(qdoc[pl.ds(t * TQ, TQ), :], (1, size // TQ)) == kdoc[:, keys_at]
        if s == back:
            query_at = lax.broadcasted_iota(jnp.int32, (TQ, 1), 0) + t * TQ
            key_at = lax.broadcasted_iota(jnp.int32, (1, size), 1) + lo
            visible = visible & (query_at >= key_at)
        for h in range(kv_heads):
            cols = pl.ds(h * HEAD, HEAD)
            scores = lax.dot_general(
                q[t, h], kbuf[keys_at, cols], (((1,), (1,)), ((), ())),
                preferred_element_type=F32,
            )
            scores = jnp.where(
                visible[None], scores.reshape(group, TQ, size), -1e30
            ).reshape(group * TQ, size)
            top = jnp.broadcast_to(
                jnp.max(scores, axis=-1, keepdims=True), (group * TQ, HEAD)
            )
            if not opens:
                older = tops[t, h]
                top = jnp.maximum(older, top)
                fade = jnp.exp2((older - top) * factor)
            weight = jnp.exp2((scores - jnp.tile(top, (1, size // HEAD))) * factor).astype(BF16)
            mixed = jnp.dot(
                weight,
                jnp.concatenate([vbuf[keys_at, cols], jnp.ones((size, HEAD), BF16)], axis=1),
                preferred_element_type=F32,
            )
            if not opens:
                mixed = acc[t, h] * jnp.tile(fade, (1, 2)) + mixed
            if closes:
                done = (mixed[:, :HEAD] / mixed[:, HEAD:]).astype(BF16)
                for g in range(group):
                    out[pl.ds(t * TQ, TQ), pl.ds((h * group + g) * HEAD, HEAD)] = done[
                        g * TQ : (g + 1) * TQ
                    ]
            else:
                acc[t, h] = mixed
                tops[t, h] = top

    def reach(t, s):
        return max(mine + (t + 1) * TQ - span - s * rows, 0)

    def final(t, s, lo):
        return lo <= reach(t, s) and all(reach(t, b) >= rows for b in range(s))

    for i, t in enumerate(reversed(range(tiles))):
        lo = reach(t, back)
        attend(t, back, lo, (t + 1) * TQ - lo, True, final(t, back, lo))
        if i % 2:
            relay(2)
    relay(len(relays))
    for s in reversed(range(1, back)):
        for t in reversed(range(tiles)):
            lo = reach(t, s)
            if lo < rows:
                attend(t, s, lo, rows - lo, False, final(t, s, lo))
    done = 0
    while done < len(last):
        for p in range(done, done + 2):
            arrived(*last[p])
        _, start, size = pieces[done]
        for t in reversed(range(tiles)):
            lo = max(reach(t, 0), start)
            if lo < start + size:
                attend(t, 0, lo, start + size - lo, False, final(t, 0, lo))
        done += 2

    for i in range(len(weights)):
        for d in range(1, n_rows):
            weight_copy(d, i).wait_send()
    for s in range(back):

        @pl.when((at >= s) & has_next)
        def _():
            for p in range(len(pieces)):
                hop(s, p).wait_send()


def solution(mesh):
    n_rows = mesh.shape["rows"]
    n_attn = mesh.shape["attn"]

    def on_device(tokens, norm_gain, w_query, w_key, w_value, documents):
        rows, width = tokens.shape
        depth, qw = w_query.shape
        kvw = w_key.shape[1]
        back = min(n_attn - 1, -(-(MOST - 1) // rows))
        block = 2 * TQ if rows % (2 * TQ) == 0 else rows
        part = 2 * HEAD if qw % (2 * HEAD) == 0 else qw
        pieces = 2 + 2 * ((rows - block) // TQ)
        table = jnp.asarray(rotary_table(documents.shape[1]))
        hbm = pl.BlockSpec(memory_space=pl.ANY)
        vmem = pl.BlockSpec(memory_space=pltpu.VMEM)
        keys = (back + 1) * rows
        group = qw // kvw
        heads = kvw // HEAD
        tiles = rows // TQ
        copies = 2 + qw // part
        args = (tokens, norm_gain, w_query, w_key, w_value, documents, table)
        return pl.pallas_call(
            functools.partial(kernel, n_rows, n_attn, back, block, part),
            out_shape=pltpu.VMEM((rows, qw), BF16),
            in_specs=[hbm, vmem, hbm, hbm, hbm, vmem, hbm],
            out_specs=vmem,
            scratch_shapes=[
                pltpu.VMEM((8, width), F32),
                pltpu.VMEM((rows, width), BF16),
                pltpu.VMEM((rows, width), BF16),
                pltpu.VMEM((n_rows, depth, 2 * kvw), BF16),
                pltpu.VMEM((qw // part, n_rows, depth, part), BF16),
                pltpu.VMEM((keys, kvw), BF16),
                pltpu.VMEM((keys, kvw), BF16),
                pltpu.VMEM((tiles, heads, group * TQ, HEAD), BF16),
                pltpu.VMEM((tiles, heads, group * TQ, HEAD), F32),
                pltpu.VMEM((tiles, heads, group * TQ, 2 * HEAD), F32),
                pltpu.VMEM((rows, HEAD), F32),
                pltpu.VMEM((1, keys), jnp.int32),
                pltpu.VMEM((rows, TQ), jnp.int32),
                pltpu.SemaphoreType.DMA((tiles,)),
                pltpu.SemaphoreType.DMA((copies + 1,)),
                pltpu.SemaphoreType.DMA((n_rows, copies)),
                pltpu.SemaphoreType.DMA((n_rows, copies)),
                pltpu.SemaphoreType.DMA((max(back, 1), pieces)),
                pltpu.SemaphoreType.DMA((max(back, 1), pieces)),
                pltpu.SemaphoreType.REGULAR,
            ],
            compiler_params=pltpu.CompilerParams(
                collective_id=0, has_side_effects=True, vmem_limit_bytes=48 << 20
            ),
            name="layer",
        )(*(pltpu.with_memory_space_constraint(a, pltpu.HBM) for a in args))

    placed = (
        P(("rows", "attn"), None),
        P(),
        P("rows", "tp"),
        P("rows", "tp"),
        P("rows", "tp"),
        P("rows", None),
    )
    return jax.shard_map(
        on_device, mesh=mesh, in_specs=placed, out_specs=P(("rows", "attn"), "tp"), check_vma=False
    )
```

```python
import functools
import math

import jax
import jax.numpy as jnp
import numpy as np
from jax import lax
from jax.experimental import pallas as pl
from jax.experimental.pallas import tpu as pltpu
from jax.sharding import PartitionSpec as P

HEAD = 128
MOST = 1024
TQ = 128
BF16 = jnp.bfloat16
F32 = jnp.float32
MESH = pl.DeviceIdType.MESH


def rotary_table(window):
    half = HEAD // 2
    frequency = np.exp(
        np.arange(half, dtype=np.float32) * np.float32(-2.0 * math.log(500000.0) / HEAD)
    ).astype(np.float32)
    angles = np.arange(window, dtype=np.float32)[:, None] * frequency[None, :]
    return np.concatenate([np.cos(angles), np.sin(angles)], axis=1).astype(np.float32)


def kernel(
    n_rows, n_attn, back, block, load,
    tok, gain_in, wq, wk, wv, docs_in, table, out,
    gain, docs, gains, xt, xn, wkv_buf, wq_buf, kbuf, vbuf, q, tops, acc, sums, qsum, tab, kdoc, qdoc,
    tok_sem, own_sem, w_send, w_recv, kv_send, kv_recv, ready,
):
    rows, width = tok.shape
    depth, kvw = wk.shape
    qw = wq.shape[1]
    kv_heads = kvw // HEAD
    group = qw // kvw
    tiles = rows // TQ
    mine = back * rows
    span = min(mine + rows, -(-(MOST - 1 + TQ) // TQ) * TQ)
    me = lax.axis_index("rows")
    at = lax.axis_index("attn")
    has_prev = at > 0
    has_next = at < n_attn - 1

    def tok_copy(c):
        here = pl.ds(c * load, load)
        return pltpu.make_async_copy(tok.at[here], xt.at[here], tok_sem.at[c])

    weights = [
        (wk, lambda d: wkv_buf.at[d, :, pl.ds(0, kvw)]),
        (wv, lambda d: wkv_buf.at[d, :, pl.ds(kvw, kvw)]),
        (wq, lambda d: wq_buf.at[d]),
    ]

    def own_copy(i):
        src, dst = weights[i]
        return pltpu.make_async_copy(src, dst(0), own_sem.at[i])

    def weight_copy(d, i):
        src, dst = weights[i]
        return pltpu.make_async_remote_copy(
            src_ref=src, dst_ref=dst(d),
            send_sem=w_send.at[d, i], recv_sem=w_recv.at[d, i],
            device_id={"rows": lax.rem(me + d, n_rows)}, device_id_type=MESH,
        )

    small = [
        pltpu.make_async_copy(src, dst, own_sem.at[len(weights) + 1 + i])
        for i, (src, dst) in enumerate(((gain_in, gain), (docs_in, docs)))
    ]
    tab_copy = pltpu.make_async_copy(
        table.at[pl.ds(pl.multiple_of(at * rows, rows), rows)], tab, own_sem.at[len(weights)]
    )

    loads = rows // load
    early = max(loads - block // load, 1)
    small[0].start()
    tok_copy(loads - 1).start()
    small[1].start()
    own_copy(0).start()
    for c in reversed(range(early, loads - 1)):
        tok_copy(c).start()
    tab_copy.start()
    own_copy(1).start()
    for c in reversed(range(min(early, loads - 1))):
        tok_copy(c).start()

    barrier = pltpu.get_barrier_semaphore()
    paired = n_rows == 2 and n_attn > 1
    if paired:
        first = me == 0

        @pl.when(jnp.logical_not(first))
        def _():
            pl.semaphore_signal(barrier, inc=1, device_id={"rows": 0}, device_id_type=MESH)

        @pl.when(first)
        def _():
            pl.semaphore_wait(barrier, 1)
            pl.semaphore_signal(ready, inc=1, device_id={"rows": 1}, device_id_type=MESH)

        @pl.when(jnp.logical_not(first))
        def _():
            pl.semaphore_wait(ready, 1)
    else:
        for d in range(1, n_rows):
            pl.semaphore_signal(
                barrier, inc=1, device_id={"rows": lax.rem(me + d, n_rows)}, device_id_type=MESH
            )
        if back:

            @pl.when(has_prev)
            def _():
                pl.semaphore_signal(
                    barrier, inc=1, device_id={"attn": at - 1}, device_id_type=MESH
                )

            pl.semaphore_wait(barrier, n_rows - 1 + has_next.astype(jnp.int32))
        elif n_rows > 1:
            pl.semaphore_wait(barrier, n_rows - 1)

    for i in range(len(weights)):
        for d in range(1, n_rows):
            weight_copy(d, i).start()
    if paired:

        @pl.when(has_prev)
        def _():
            pl.semaphore_signal(
                barrier, inc=1, device_id={"rows": 1, "attn": at - 1}, device_id_type=MESH
            )

    for i in range(2, len(weights)):
        own_copy(i).start()

    small[1].wait()
    for s in range(back + 1):
        owner = at - back + s
        keep = pl.multiple_of(jnp.maximum(owner, 0) * rows, rows)
        kdoc[:, pl.ds(s * rows, rows)] = jnp.where(owner >= 0, docs[:, pl.ds(keep, rows)], -1)
    for t in range(tiles):
        row = kdoc[:, pl.ds(mine + t * TQ, TQ)]
        qdoc[pl.ds(t * TQ, TQ), :] = jnp.broadcast_to(row, (TQ, TQ)).T
    for s in range(back):

        @pl.when(at - back + s < 0)
        def _():
            kbuf[pl.ds(s * rows, rows), :] = jnp.zeros((rows, kvw), BF16)
            vbuf[pl.ds(s * rows, rows), :] = jnp.zeros((rows, kvw), BF16)

    small[0].wait()
    gains[...] = jnp.broadcast_to(gain[...].astype(F32).reshape(1, -1), gains.shape)

    pieces = [(which, rows - block, block) for which in range(2)]
    for c in reversed(range((rows - block) // TQ)):
        pieces += [(which, c * TQ, TQ) for which in range(2)]

    def hop(s, p):
        which, start, size = pieces[p]
        ref = (kbuf, vbuf)[which]
        return pltpu.make_async_remote_copy(
            src_ref=ref.at[pl.ds((back - s) * rows + start, size)],
            dst_ref=ref.at[pl.ds((back - s - 1) * rows + start, size)],
            send_sem=kv_send.at[s, p], recv_sem=kv_recv.at[s, p],
            device_id={"attn": jnp.minimum(at + 1, n_attn - 1)}, device_id_type=MESH,
        )

    def send(wanted):
        if back:

            @pl.when(has_next)
            def _():
                for p in wanted:
                    hop(0, p).start()

    def arrived(s, p):
        @pl.when(at > s)
        def _():
            hop(s, p).wait_recv()

        if s + 1 < back:

            @pl.when((at > s) & has_next)
            def _():
                hop(s + 1, p).start()

    relays = [(s, p) for s in range(back - 1) for p in range(len(pieces))]
    last = [(back - 1, p) for p in range(len(pieces))] if back else []

    def relay(count):
        for _ in range(min(count, len(relays))):
            arrived(*relays.pop(0))

    strip, piece = 16, 256

    def norm(c):
        @pl.loop(0, load // strip, unroll=4)
        def _(i):
            here = pl.ds(pl.multiple_of(c * load + i * strip, strip), strip)
            squares = jnp.zeros((strip, piece), F32)
            for k in range(width // piece):
                x = xt[here, pl.ds(k * piece, piece)].astype(F32)
                squares = squares + x * x
            mean_sq = jnp.sum(squares, axis=-1, keepdims=True) * (1.0 / width)
            scale = jnp.broadcast_to(lax.rsqrt(mean_sq + 1e-05), (strip, piece))
            for k in range(width // piece):
                cols = pl.ds(k * piece, piece)
                x = xt[here, cols].astype(F32) * scale
                xn[here, cols] = (
                    x.reshape(strip // 8, 8, piece) * gains[:, cols][None]
                ).reshape(strip, piece).astype(BF16)

    lane = lax.broadcasted_iota(jnp.int32, (1, HEAD), 1)

    def tables(start, size):
        t = tab[pl.ds(start, size), :]
        swapped = pltpu.roll(t, HEAD // 2, 1)
        low = lane < HEAD // 2
        return jnp.where(low, t, swapped), jnp.where(low, -swapped, t)

    def rotate(u, cosine, sine):
        return (u * cosine + pltpu.roll(u, HEAD // 2, 1) * sine).astype(BF16)

    half = depth // 2 if depth % (2 * HEAD) == 0 else depth

    def dots(start, size, terms, weight):
        total = None
        for d, k in terms:
            owner = lax.rem(me - d + n_rows, n_rows)
            here = pl.ds(pl.multiple_of(owner * depth + k, half), half)
            term = jnp.dot(
                xn[pl.ds(start, size), here], weight(d, k), preferred_element_type=F32
            )
            total = term if total is None else total + term
        return total

    def project(start, size, first_col, cols):
        def weight(d, k):
            return wkv_buf[d, pl.ds(k, half), pl.ds(first_col, cols)]

        terms = [(d, k) for d in range(n_rows) for k in range(0, depth, half)]
        for chain in range(2):
            sums[chain, pl.ds(0, size), pl.ds(0, cols)] = dots(
                start, size, terms[chain::2], weight
            )
        return sums[0, pl.ds(0, size), pl.ds(0, cols)] + sums[1, pl.ds(0, size), pl.ds(0, cols)]

    def store_keys(start, size, total):
        cosine, sine = tables(start, size)
        for h in range(kv_heads):
            cols = pl.ds(h * HEAD, HEAD)
            kbuf[pl.ds(mine + start, size), cols] = rotate(
                total[:, h * HEAD : (h + 1) * HEAD], cosine, sine
            )

    def store_values(start, size, total):
        vbuf[pl.ds(mine + start, size), :] = total.astype(BF16)

    high = rows - block
    for c in reversed(range(high // load, loads)):
        tok_copy(c).wait()
        norm(c)
    tab_copy.wait()

    def weight_ready(i):
        own_copy(i).wait()
        for d in range(1, n_rows):
            weight_copy(d, i).wait_recv()

    weight_ready(0)
    total = project(high, block, 0, kvw)
    if paired:

        @pl.when(has_next & jnp.logical_not(first))
        def _():
            pl.semaphore_wait(barrier, 2)
            pl.semaphore_signal(ready, inc=1, device_id={"rows": 0}, device_id_type=MESH)

    store_keys(high, block, total)
    if paired:

        @pl.when(has_next & first)
        def _():
            pl.semaphore_wait(ready, 1)

    send([0])
    for c in reversed(range(high // load)):
        tok_copy(c).wait()
    weight_ready(1)
    store_values(high, block, project(high, block, kvw, kvw))
    for c in reversed(range(high // load)):
        norm(c)
    send([1])
    sent = 2
    for b in reversed(range(high // block)):
        total = project(b * block, block, 0, 2 * kvw)
        store_keys(b * block, block, total[:, :kvw])
        store_values(b * block, block, total[:, kvw:])
        count = 2 * (block // TQ)
        send(range(sent, sent + count))
        sent += count

    def queries(start, d):
        owner = lax.rem(me - d + n_rows, n_rows)
        here = pl.ds(pl.multiple_of(owner * depth, depth), depth)
        return jnp.dot(xn[pl.ds(start, block), here], wq_buf[d], preferred_element_type=F32)

    steps = [b * block for b in reversed(range(rows // block))]
    own_copy(2).wait()
    for start in steps:
        qsum[pl.ds(start, block), :] = queries(start, 0)
    relay(1)
    for d in range(1, n_rows):
        weight_copy(d, 2).wait_recv()
    for start in steps:
        total = qsum[pl.ds(start, block), :]
        for d in range(1, n_rows):
            total = total + queries(start, d)
        cosine, sine = tables(start, block)
        for h in range(kv_heads):
            for g in range(group):
                col = (h * group + g) * HEAD
                u = rotate(total[:, col : col + HEAD], cosine, sine)
                for t in range(block // TQ):
                    q[start // TQ + t, h, pl.ds(g * TQ, TQ), :] = u[t * TQ : (t + 1) * TQ]
    relay(1)

    factor = math.log2(math.e) / math.sqrt(HEAD)

    def attend(t, s, lo, size, opens, closes):
        seen = s * rows + lo
        keys_at = pl.ds(seen, size)
        visible = jnp.tile(qdoc[pl.ds(t * TQ, TQ), :], (1, size // TQ)) == kdoc[:, keys_at]
        if s == back:
            query_at = lax.broadcasted_iota(jnp.int32, (TQ, 1), 0) + t * TQ
            key_at = lax.broadcasted_iota(jnp.int32, (1, size), 1) + lo
            visible = visible & (query_at >= key_at)
        for h in range(kv_heads):
            cols = pl.ds(h * HEAD, HEAD)
            scores = lax.dot_general(
                q[t, h], kbuf[keys_at, cols], (((1,), (1,)), ((), ())),
                preferred_element_type=F32,
            )
            scores = jnp.where(
                visible[None], scores.reshape(group, TQ, size), -1e30
            ).reshape(group * TQ, size)
            top = jnp.broadcast_to(
                jnp.max(scores, axis=-1, keepdims=True), (group * TQ, HEAD)
            )
            if not opens:
                older = tops[t, h]
                top = jnp.maximum(older, top)
                fade = jnp.exp2((older - top) * factor)
            weight = jnp.exp2((scores - jnp.tile(top, (1, size // HEAD))) * factor).astype(BF16)
            mixed = jnp.dot(
                weight,
                jnp.concatenate([vbuf[keys_at, cols], jnp.ones((size, HEAD), BF16)], axis=1),
                preferred_element_type=F32,
            )
            if not opens:
                mixed = acc[t, h] * jnp.tile(fade, (1, 2)) + mixed
            if closes:
                done = (mixed[:, :HEAD] / mixed[:, HEAD:]).astype(BF16)
                for g in range(group):
                    out[pl.ds(t * TQ, TQ), pl.ds((h * group + g) * HEAD, HEAD)] = done[
                        g * TQ : (g + 1) * TQ
                    ]
            else:
                acc[t, h] = mixed
                tops[t, h] = top

    def reach(t, s):
        return max(mine + (t + 1) * TQ - span - s * rows, 0)

    def final(t, s, lo):
        return lo <= reach(t, s) and all(reach(t, b) >= rows for b in range(s))

    for i, t in enumerate(reversed(range(tiles))):
        lo = reach(t, back)
        attend(t, back, lo, (t + 1) * TQ - lo, True, final(t, back, lo))
        if i % 2:
            relay(2)
    relay(len(relays))
    for s in reversed(range(1, back)):
        for t in reversed(range(tiles)):
            lo = reach(t, s)
            if lo < rows:
                attend(t, s, lo, rows - lo, False, final(t, s, lo))
    for i in range(len(weights)):
        for d in range(1, n_rows):
            weight_copy(d, i).wait_send()
    done = 0
    while done < len(last):
        if done + 2 >= len(last):
            for s in range(back):

                @pl.when((at >= s) & has_next)
                def _():
                    for p in range(len(pieces)):
                        hop(s, p).wait_send()

        for p in range(done, done + 2):
            arrived(*last[p])
        _, start, size = pieces[done]
        for t in reversed(range(tiles)):
            lo = max(reach(t, 0), start)
            if lo < start + size:
                attend(t, 0, lo, start + size - lo, False, final(t, 0, lo))
        done += 2


def solution(mesh):
    n_rows = mesh.shape["rows"]
    n_attn = mesh.shape["attn"]

    def on_device(tokens, norm_gain, w_query, w_key, w_value, documents):
        rows, width = tokens.shape
        depth, qw = w_query.shape
        kvw = w_key.shape[1]
        back = min(n_attn - 1, -(-(MOST - 1) // rows))
        block = 2 * TQ if rows % (2 * TQ) == 0 else rows
        load = TQ // 2
        pieces = 2 + 2 * ((rows - block) // TQ)
        table = jnp.asarray(rotary_table(documents.shape[1]))
        hbm = pl.BlockSpec(memory_space=pl.ANY)
        vmem = pl.BlockSpec(memory_space=pltpu.VMEM)
        keys = (back + 1) * rows
        group = qw // kvw
        heads = kvw // HEAD
        tiles = rows // TQ
        copies = 3
        args = (tokens, norm_gain, w_query, w_key, w_value, documents, table)
        return pl.pallas_call(
            functools.partial(kernel, n_rows, n_attn, back, block, load),
            out_shape=pltpu.VMEM((rows, qw), BF16),
            in_specs=[hbm] * len(args),
            out_specs=vmem,
            scratch_shapes=[
                pltpu.VMEM((width,), BF16),
                pltpu.VMEM(documents.shape, jnp.int32),
                pltpu.VMEM((8, width), F32),
                pltpu.VMEM((rows, width), BF16),
                pltpu.VMEM((rows, width), BF16),
                pltpu.VMEM((n_rows, depth, 2 * kvw), BF16),
                pltpu.VMEM((n_rows, depth, qw), BF16),
                pltpu.VMEM((keys, kvw), BF16),
                pltpu.VMEM((keys, kvw), BF16),
                pltpu.VMEM((tiles, heads, group * TQ, HEAD), BF16),
                pltpu.VMEM((tiles, heads, group * TQ, HEAD), F32),
                pltpu.VMEM((tiles, heads, group * TQ, 2 * HEAD), F32),
                pltpu.VMEM((2, block, 2 * kvw), F32),
                pltpu.VMEM((rows, qw), F32),
                pltpu.VMEM((rows, HEAD), F32),
                pltpu.VMEM((1, keys), jnp.int32),
                pltpu.VMEM((rows, TQ), jnp.int32),
                pltpu.SemaphoreType.DMA((rows // load,)),
                pltpu.SemaphoreType.DMA((copies + 3,)),
                pltpu.SemaphoreType.DMA((n_rows, copies)),
                pltpu.SemaphoreType.DMA((n_rows, copies)),
                pltpu.SemaphoreType.DMA((max(back, 1), pieces)),
                pltpu.SemaphoreType.DMA((max(back, 1), pieces)),
                pltpu.SemaphoreType.REGULAR,
            ],
            compiler_params=pltpu.CompilerParams(
                collective_id=0, has_side_effects=True, vmem_limit_bytes=48 << 20
            ),
            name="layer",
        )(*(pltpu.with_memory_space_constraint(a, pltpu.HBM) for a in args))

    placed = (
        P(("rows", "attn"), None),
        P(),
        P("rows", "tp"),
        P("rows", "tp"),
        P("rows", "tp"),
        P("rows", None),
    )
    return jax.shard_map(
        on_device, mesh=mesh, in_specs=placed, out_specs=P(("rows", "attn"), "tp"), check_vma=False
    )
```

```python
import functools
import math

import jax
import jax.numpy as jnp
import numpy as np
from jax import lax
from jax.experimental import pallas as pl
from jax.experimental.pallas import tpu as pltpu
from jax.sharding import PartitionSpec as P

HEAD = 128
MOST = 1024
TQ = 128
BF16 = jnp.bfloat16
F32 = jnp.float32
MESH = pl.DeviceIdType.MESH


def rotary_table(window):
    half = HEAD // 2
    frequency = np.exp(
        np.arange(half, dtype=np.float32) * np.float32(-2.0 * math.log(500000.0) / HEAD)
    ).astype(np.float32)
    angles = np.arange(window, dtype=np.float32)[:, None] * frequency[None, :]
    return np.concatenate([np.cos(angles), np.sin(angles)], axis=1).astype(np.float32)


def kernel(
    n_rows, n_attn, back, block, load,
    tok, gain_in, wq, wk, wv, docs_in, table, out,
    gain, docs, gains, xt, xn, wkv_buf, wq_buf, kbuf, vbuf, q, tops, acc, sums, qsum, tab, kdoc, qdoc,
    tok_sem, own_sem, w_send, w_recv, kv_send, kv_recv, ready,
):
    rows, width = tok.shape
    depth, kvw = wk.shape
    qw = wq.shape[1]
    kv_heads = kvw // HEAD
    group = qw // kvw
    tiles = rows // TQ
    mine = back * rows
    span = min(mine + rows, -(-(MOST - 1 + TQ) // TQ) * TQ)
    me = lax.axis_index("rows")
    at = lax.axis_index("attn")
    has_prev = at > 0
    has_next = at < n_attn - 1

    def tok_copy(c):
        here = pl.ds(c * load, load)
        return pltpu.make_async_copy(tok.at[here], xt.at[here], tok_sem.at[c])

    weights = [
        (wk, lambda d: wkv_buf.at[d, :, pl.ds(0, kvw)]),
        (wv, lambda d: wkv_buf.at[d, :, pl.ds(kvw, kvw)]),
        (wq, lambda d: wq_buf.at[d]),
    ]

    def own_copy(i):
        src, dst = weights[i]
        return pltpu.make_async_copy(src, dst(0), own_sem.at[i])

    def weight_copy(d, i):
        src, dst = weights[i]
        return pltpu.make_async_remote_copy(
            src_ref=src, dst_ref=dst(d),
            send_sem=w_send.at[d, i], recv_sem=w_recv.at[d, i],
            device_id={"rows": lax.rem(me + d, n_rows)}, device_id_type=MESH,
        )

    small = [
        pltpu.make_async_copy(src, dst, own_sem.at[len(weights) + 1 + i])
        for i, (src, dst) in enumerate(((gain_in, gain), (docs_in, docs)))
    ]
    tab_copy = pltpu.make_async_copy(
        table.at[pl.ds(pl.multiple_of(at * rows, rows), rows)], tab, own_sem.at[len(weights)]
    )

    loads = rows // load
    early = loads - block // load
    small[0].start()
    for c in reversed(range(early, loads)):
        tok_copy(c).start()
        if c == max(loads - 2, early):
            own_copy(0).start()
    tab_copy.start()

    barrier = pltpu.get_barrier_semaphore()
    paired = n_rows == 2 and n_attn > 1
    if paired:
        first = me == 0

        @pl.when(jnp.logical_not(first))
        def _():
            pl.semaphore_signal(barrier, inc=1, device_id={"rows": 0}, device_id_type=MESH)

        @pl.when(first)
        def _():
            pl.semaphore_wait(barrier, 1)
            pl.semaphore_signal(ready, inc=1, device_id={"rows": 1}, device_id_type=MESH)

        @pl.when(jnp.logical_not(first))
        def _():
            pl.semaphore_wait(ready, 1)
    else:
        for d in range(1, n_rows):
            pl.semaphore_signal(
                barrier, inc=1, device_id={"rows": lax.rem(me + d, n_rows)}, device_id_type=MESH
            )
        if back:

            @pl.when(has_prev)
            def _():
                pl.semaphore_signal(
                    barrier, inc=1, device_id={"attn": at - 1}, device_id_type=MESH
                )

            pl.semaphore_wait(barrier, n_rows - 1 + has_next.astype(jnp.int32))
        elif n_rows > 1:
            pl.semaphore_wait(barrier, n_rows - 1)

    for i in range(2):
        for d in range(1, n_rows):
            weight_copy(d, i).start()
    if paired:

        @pl.when(has_prev)
        def _():
            pl.semaphore_signal(
                barrier, inc=1, device_id={"rows": 1, "attn": at - 1}, device_id_type=MESH
            )

    for s in range(back):

        @pl.when(at - back + s < 0)
        def _():
            kbuf[pl.ds(s * rows, rows), :] = jnp.zeros((rows, kvw), BF16)
            vbuf[pl.ds(s * rows, rows), :] = jnp.zeros((rows, kvw), BF16)

    upper = block // TQ
    pieces = [
        (which, c * TQ, TQ)
        for b in reversed(range(rows // block))
        for which in range(2)
        for c in reversed(range(b * upper, (b + 1) * upper))
    ]

    def hop(s, p):
        which, start, size = pieces[p]
        ref = (kbuf, vbuf)[which]
        return pltpu.make_async_remote_copy(
            src_ref=ref.at[pl.ds((back - s) * rows + start, size)],
            dst_ref=ref.at[pl.ds((back - s - 1) * rows + start, size)],
            send_sem=kv_send.at[s, p], recv_sem=kv_recv.at[s, p],
            device_id={"attn": jnp.minimum(at + 1, n_attn - 1)}, device_id_type=MESH,
        )

    def send(wanted):
        if back:

            @pl.when(has_next)
            def _():
                for p in wanted:
                    hop(0, p).start()

    def arrived(s, p):
        @pl.when(at > s)
        def _():
            hop(s, p).wait_recv()

        if s + 1 < back:

            @pl.when((at > s) & has_next)
            def _():
                hop(s + 1, p).start()

    relays = [(s, p) for s in range(back - 1) for p in range(len(pieces))]
    last = [(back - 1, p) for p in range(len(pieces))] if back else []

    def relay(count):
        for _ in range(min(count, len(relays))):
            arrived(*relays.pop(0))

    strip, piece = 16, 256

    def norm(c):
        @pl.loop(0, load // strip, unroll=4)
        def _(i):
            here = pl.ds(pl.multiple_of(c * load + i * strip, strip), strip)
            squares = jnp.zeros((strip, piece), F32)
            for k in range(width // piece):
                x = xt[here, pl.ds(k * piece, piece)].astype(F32)
                squares = squares + x * x
            mean_sq = jnp.sum(squares, axis=-1, keepdims=True) * (1.0 / width)
            scale = jnp.broadcast_to(lax.rsqrt(mean_sq + 1e-05), (strip, piece))
            for k in range(width // piece):
                cols = pl.ds(k * piece, piece)
                x = xt[here, cols].astype(F32) * scale
                xn[here, cols] = (
                    x.reshape(strip // 8, 8, piece) * gains[:, cols][None]
                ).reshape(strip, piece).astype(BF16)

    lane = lax.broadcasted_iota(jnp.int32, (1, HEAD), 1)

    def tables(start, size):
        t = tab[pl.ds(start, size), :]
        swapped = pltpu.roll(t, HEAD // 2, 1)
        low = lane < HEAD // 2
        return jnp.where(low, t, swapped), jnp.where(low, -swapped, t)

    def rotate(u, cosine, sine):
        return (u * cosine + pltpu.roll(u, HEAD // 2, 1) * sine).astype(BF16)

    half = depth // 2 if depth % (2 * HEAD) == 0 else depth

    def dots(start, size, terms, weight):
        total = None
        for d, k in terms:
            owner = lax.rem(me - d + n_rows, n_rows)
            here = pl.ds(pl.multiple_of(owner * depth + k, half), half)
            term = jnp.dot(
                xn[pl.ds(start, size), here], weight(d, k), preferred_element_type=F32
            )
            total = term if total is None else total + term
        return total

    def project(start, size, first_col, cols):
        def weight(d, k):
            return wkv_buf[d, pl.ds(k, half), pl.ds(first_col, cols)]

        terms = [(d, k) for d in range(n_rows) for k in range(0, depth, half)]
        for chain in range(2):
            sums[chain, pl.ds(0, size), pl.ds(0, cols)] = dots(
                start, size, terms[chain::2], weight
            )
        return sums[0, pl.ds(0, size), pl.ds(0, cols)] + sums[1, pl.ds(0, size), pl.ds(0, cols)]

    def store_keys(start, size, total):
        cosine, sine = tables(start, size)
        for h in range(kv_heads):
            cols = pl.ds(h * HEAD, HEAD)
            kbuf[pl.ds(mine + start, size), cols] = rotate(
                total[:, h * HEAD : (h + 1) * HEAD], cosine, sine
            )

    def store_values(start, size, total):
        vbuf[pl.ds(mine + start, size), :] = total.astype(BF16)

    high = rows - block
    per = TQ // load

    def norm_chunk(c):
        for i in reversed(range(c * per, (c + 1) * per)):
            norm(i)

    def tok_wait(c):
        for i in reversed(range(c * per, (c + 1) * per)):
            tok_copy(i).wait()

    def weight_ready(i):
        for d in range(1, n_rows):
            weight_copy(d, i).wait_recv()

    for c in reversed(range(high // TQ, tiles)):
        tok_wait(c)
        if c == tiles - 1:
            small[0].wait()
            gains[...] = jnp.broadcast_to(gain[...].astype(F32).reshape(1, -1), gains.shape)
        norm_chunk(c)
        if c == tiles - 1:
            own_copy(1).start()
            for i in reversed(range(early)):
                tok_copy(i).start()
            for d in range(1, n_rows):
                weight_copy(d, 2).start()
            small[1].start()
            own_copy(2).start()
    tab_copy.wait()
    own_copy(0).wait()
    key_cols = pl.ds(0, kvw)

    def key_weight(d, k):
        return wkv_buf[d, pl.ds(k, half), key_cols]

    own = [(0, k) for k in range(0, depth, half)]
    for chain in range(2):
        sums[chain, :, key_cols] = (
            dots(high, block, own[chain::2], key_weight)
            if own[chain::2]
            else jnp.zeros((block, kvw), F32)
        )
    weight_ready(0)
    far = [(d, k) for d in range(1, n_rows) for k in range(0, depth, half)]
    for i in range(upper):
        start = rows - (i + 1) * TQ
        here = pl.ds(start - high, TQ)
        for chain in range(2):
            if far[chain::2]:
                sums[chain, here, key_cols] = sums[chain, here, key_cols] + dots(
                    start, TQ, far[chain::2], key_weight
                )
        store_keys(start, TQ, sums[0, here, key_cols] + sums[1, here, key_cols])
        if i == 0 and paired:

            @pl.when(has_next & jnp.logical_not(first))
            def _():
                pl.semaphore_wait(barrier, 2)
                pl.semaphore_signal(ready, inc=1, device_id={"rows": 0}, device_id_type=MESH)

            @pl.when(has_next & first)
            def _():
                pl.semaphore_wait(ready, 1)

        send([i])
    own_copy(1).wait()
    weight_ready(1)
    store_values(high, block, project(high, block, kvw, kvw))
    send(range(upper, 2 * upper))
    for c in reversed(range(high // TQ)):
        tok_wait(c)
    for c in reversed(range(high // TQ)):
        norm_chunk(c)
    sent = 2 * upper
    for b in reversed(range(high // block)):
        store_keys(b * block, block, project(b * block, block, 0, kvw))
        send(range(sent, sent + upper))
        store_values(b * block, block, project(b * block, block, kvw, kvw))
        send(range(sent + upper, sent + 2 * upper))
        sent += 2 * upper
    small[1].wait()
    for s in range(back + 1):
        owner = at - back + s
        keep = pl.multiple_of(jnp.maximum(owner, 0) * rows, rows)
        kdoc[:, pl.ds(s * rows, rows)] = jnp.where(owner >= 0, docs[:, pl.ds(keep, rows)], -1)
    for t in range(tiles):
        row = kdoc[:, pl.ds(mine + t * TQ, TQ)]
        qdoc[pl.ds(t * TQ, TQ), :] = jnp.broadcast_to(row, (TQ, TQ)).T

    def queries(start, d):
        owner = lax.rem(me - d + n_rows, n_rows)
        here = pl.ds(pl.multiple_of(owner * depth, depth), depth)
        return jnp.dot(xn[pl.ds(start, block), here], wq_buf[d], preferred_element_type=F32)

    steps = [b * block for b in reversed(range(rows // block))]
    own_copy(2).wait()
    for start in steps:
        qsum[pl.ds(start, block), :] = queries(start, 0)
    relay(2)
    for d in range(1, n_rows):
        weight_copy(d, 2).wait_recv()
    for start in steps:
        total = qsum[pl.ds(start, block), :]
        for d in range(1, n_rows):
            total = total + queries(start, d)
        cosine, sine = tables(start, block)
        for h in range(kv_heads):
            for g in range(group):
                col = (h * group + g) * HEAD
                u = rotate(total[:, col : col + HEAD], cosine, sine)
                for t in range(block // TQ):
                    q[start // TQ + t, h, pl.ds(g * TQ, TQ), :] = u[t * TQ : (t + 1) * TQ]
    relay(2)

    factor = math.log2(math.e) / math.sqrt(HEAD)

    def weigh(t, s, lo, size, opens):
        seen = s * rows + lo
        keys_at = pl.ds(seen, size)
        visible = jnp.tile(qdoc[pl.ds(t * TQ, TQ), :], (1, size // TQ)) == kdoc[:, keys_at]
        if s == back:
            query_at = lax.broadcasted_iota(jnp.int32, (TQ, 1), 0) + t * TQ
            key_at = lax.broadcasted_iota(jnp.int32, (1, size), 1) + lo
            visible = visible & (query_at >= key_at)
        made = []
        for h in range(kv_heads):
            scores = lax.dot_general(
                q[t, h], kbuf[keys_at, pl.ds(h * HEAD, HEAD)], (((1,), (1,)), ((), ())),
                preferred_element_type=F32,
            )
            scores = jnp.where(
                visible[None], scores.reshape(group, TQ, size), -1e30
            ).reshape(group * TQ, size)
            top = jnp.broadcast_to(
                jnp.max(scores, axis=-1, keepdims=True), (group * TQ, HEAD)
            )
            fade = None
            if not opens:
                older = tops[t, h]
                top = jnp.maximum(older, top)
                fade = jnp.exp2((older - top) * factor)
            weight = jnp.exp2((scores - jnp.tile(top, (1, size // HEAD))) * factor).astype(BF16)
            made.append((weight, fade))
            tops[t, h] = top
        return made

    def mix(t, s, lo, size, made, closes):
        keys_at = pl.ds(s * rows + lo, size)
        for h in range(kv_heads):
            weight, fade = made[h]
            mixed = jnp.dot(
                weight,
                jnp.concatenate(
                    [vbuf[keys_at, pl.ds(h * HEAD, HEAD)], jnp.ones((size, HEAD), BF16)], axis=1
                ),
                preferred_element_type=F32,
            )
            if fade is not None:
                mixed = acc[t, h] * jnp.tile(fade, (1, 2)) + mixed
            if closes:
                done = (mixed[:, :HEAD] / mixed[:, HEAD:]).astype(BF16)
                for g in range(group):
                    out[pl.ds(t * TQ, TQ), pl.ds((h * group + g) * HEAD, HEAD)] = done[
                        g * TQ : (g + 1) * TQ
                    ]
            else:
                acc[t, h] = mixed

    def attend(t, s, lo, size, opens, closes):
        mix(t, s, lo, size, weigh(t, s, lo, size, opens), closes)

    def reach(t, s):
        return max(mine + (t + 1) * TQ - span - s * rows, 0)

    def final(t, s, lo):
        return lo <= reach(t, s) and all(reach(t, b) >= rows for b in range(s))

    for i, t in enumerate(reversed(range(tiles))):
        lo = reach(t, back)
        attend(t, back, lo, (t + 1) * TQ - lo, True, final(t, back, lo))
        if i % 2:
            relay(2)
    relay(len(relays))
    for s in reversed(range(1, back)):
        for t in reversed(range(tiles)):
            lo = reach(t, s)
            if lo < rows:
                attend(t, s, lo, rows - lo, False, final(t, s, lo))
    for i in range(len(weights)):
        for d in range(1, n_rows):
            weight_copy(d, i).wait_send()
    def come(which, start, size):
        for s, p in last:
            if pieces[p][0] == which and start <= pieces[p][1] < start + size:
                arrived(s, p)

    def sent_all():
        for s in range(back):

            @pl.when((at >= s) & has_next)
            def _():
                for p in range(len(pieces)):
                    hop(s, p).wait_send()

    blocks = list(reversed(range(0, rows, block))) if back else []
    for start in blocks:
        end = start + block
        low = {t: max(reach(t, 0), start) for t in reversed(range(tiles))}
        low = {t: lo for t, lo in low.items() if lo < end}
        if start == high and start > 0:
            come(0, start, block)
            made = {t: weigh(t, 0, lo, end - lo, False) for t, lo in low.items()}
            come(1, start, block)
            for t, lo in low.items():
                mix(t, 0, lo, end - lo, made[t], final(t, 0, lo))
            continue
        pairs = [(t, h) for t in low for h in range(kv_heads)]
        base = {(t, h): acc[t, h][:, :HEAD] for t, h in pairs}
        total = {(t, h): acc[t, h][:, HEAD:] for t, h in pairs}
        made = {}
        for c in reversed(range(start, end, TQ)):
            come(0, c, TQ)
            for t, lo in low.items():
                if lo > c:
                    continue
                for h, (weight, fade) in enumerate(weigh(t, 0, c, TQ, False)):
                    for e in range(c + TQ, end, TQ):
                        older, carry = made[t, h, e]
                        made[t, h, e] = older, fade if carry is None else carry * fade
                    made[t, h, c] = weight, None
                    base[t, h] = base[t, h] * fade
                    total[t, h] = total[t, h] * fade + jnp.dot(
                        weight, jnp.ones((TQ, HEAD), BF16), preferred_element_type=F32
                    )
                    if c == lo and final(t, 0, lo):
                        total[t, h] = 1.0 / total[t, h]
        for c in reversed(range(start, end, TQ)):
            if c == 0:
                sent_all()
            come(1, c, TQ)
            for t, h in pairs:
                if low[t] > c:
                    continue
                weight, carry = made[t, h, c]
                fresh = jnp.dot(
                    weight, vbuf[pl.ds(c, TQ), pl.ds(h * HEAD, HEAD)],
                    preferred_element_type=F32,
                )
                base[t, h] = base[t, h] + (fresh if carry is None else fresh * carry)
                if low[t] < c:
                    continue
                if final(t, 0, low[t]):
                    done = (base[t, h] * total[t, h]).astype(BF16)
                    for g in range(group):
                        out[pl.ds(t * TQ, TQ), pl.ds((h * group + g) * HEAD, HEAD)] = done[
                            g * TQ : (g + 1) * TQ
                        ]
                else:
                    acc[t, h] = jnp.concatenate([base[t, h], total[t, h]], axis=1)


def solution(mesh):
    n_rows = mesh.shape["rows"]
    n_attn = mesh.shape["attn"]

    def on_device(tokens, norm_gain, w_query, w_key, w_value, documents):
        rows, width = tokens.shape
        depth, qw = w_query.shape
        kvw = w_key.shape[1]
        back = min(n_attn - 1, -(-(MOST - 1) // rows))
        block = 2 * TQ if rows % (2 * TQ) == 0 else rows
        load = TQ // 2
        pieces = 2 * (rows // TQ)
        table = jnp.asarray(rotary_table(documents.shape[1]))
        hbm = pl.BlockSpec(memory_space=pl.ANY)
        vmem = pl.BlockSpec(memory_space=pltpu.VMEM)
        keys = (back + 1) * rows
        group = qw // kvw
        heads = kvw // HEAD
        tiles = rows // TQ
        copies = 3
        args = (tokens, norm_gain, w_query, w_key, w_value, documents, table)
        return pl.pallas_call(
            functools.partial(kernel, n_rows, n_attn, back, block, load),
            out_shape=pltpu.VMEM((rows, qw), BF16),
            in_specs=[hbm] * len(args),
            out_specs=vmem,
            scratch_shapes=[
                pltpu.VMEM((width,), BF16),
                pltpu.VMEM(documents.shape, jnp.int32),
                pltpu.VMEM((8, width), F32),
                pltpu.VMEM((rows, width), BF16),
                pltpu.VMEM((rows, width), BF16),
                pltpu.VMEM((n_rows, depth, 2 * kvw), BF16),
                pltpu.VMEM((n_rows, depth, qw), BF16),
                pltpu.VMEM((keys, kvw), BF16),
                pltpu.VMEM((keys, kvw), BF16),
                pltpu.VMEM((tiles, heads, group * TQ, HEAD), BF16),
                pltpu.VMEM((tiles, heads, group * TQ, HEAD), F32),
                pltpu.VMEM((tiles, heads, group * TQ, 2 * HEAD), F32),
                pltpu.VMEM((2, block, 2 * kvw), F32),
                pltpu.VMEM((rows, qw), F32),
                pltpu.VMEM((rows, HEAD), F32),
                pltpu.VMEM((1, keys), jnp.int32),
                pltpu.VMEM((rows, TQ), jnp.int32),
                pltpu.SemaphoreType.DMA((rows // load,)),
                pltpu.SemaphoreType.DMA((copies + 3,)),
                pltpu.SemaphoreType.DMA((n_rows, copies)),
                pltpu.SemaphoreType.DMA((n_rows, copies)),
                pltpu.SemaphoreType.DMA((max(back, 1), pieces)),
                pltpu.SemaphoreType.DMA((max(back, 1), pieces)),
                pltpu.SemaphoreType.REGULAR,
            ],
            compiler_params=pltpu.CompilerParams(
                collective_id=0, has_side_effects=True, vmem_limit_bytes=48 << 20
            ),
            name="layer",
        )(*(pltpu.with_memory_space_constraint(a, pltpu.HBM) for a in args))

    placed = (
        P(("rows", "attn"), None),
        P(),
        P("rows", "tp"),
        P("rows", "tp"),
        P("rows", "tp"),
        P("rows", None),
    )
    return jax.shard_map(
        on_device, mesh=mesh, in_specs=placed, out_specs=P(("rows", "attn"), "tp"), check_vma=False
    )
```

```python
import functools
import math

import jax
import jax.numpy as jnp
import numpy as np
from jax import lax
from jax.experimental import pallas as pl
from jax.experimental.pallas import tpu as pltpu
from jax.sharding import PartitionSpec as P

HEAD = 128
MOST = 1024
TQ = 128
BF16 = jnp.bfloat16
F32 = jnp.float32
MESH = pl.DeviceIdType.MESH


def rotary_table(window):
    half = HEAD // 2
    frequency = np.exp(
        np.arange(half, dtype=np.float32) * np.float32(-2.0 * math.log(500000.0) / HEAD)
    ).astype(np.float32)
    angles = np.arange(window, dtype=np.float32)[:, None] * frequency[None, :]
    return np.concatenate([np.cos(angles), np.sin(angles)], axis=1).astype(np.float32)


def hop_copies(rows, block, back):
    copies = []
    for s in range(back):
        unit = 0
        for b in reversed(range(rows // block)):
            for which in range(2):
                upper = b == rows // block - 1
                fine = (upper and which == 0) if s == 0 else (s == back - 1 and not upper)
                size = TQ if fine else block
                for start in reversed(range(b * block, (b + 1) * block, size)):
                    copies.append((s, unit, which, start, size))
                unit += 1
    return copies


def kernel(
    n_rows, n_attn, back, block,
    tok, gain_in, wq, wk, wv, docs_in, table, out,
    gain, docs, gains, xt, xn, wkv_buf, wq_buf, kbuf, vbuf, q, tops, acc, sums, qsum, tab, kdoc, qdoc,
    own_sem, w_send, w_recv, kv_send, kv_recv, ready,
):
    rows, width = tok.shape
    depth, kvw = wk.shape
    qw = wq.shape[1]
    kv_heads = kvw // HEAD
    group = qw // kvw
    tiles = rows // TQ
    mine = back * rows
    span = min(mine + rows, -(-(MOST - 1 + TQ) // TQ) * TQ)
    me = lax.axis_index("rows")
    at = lax.axis_index("attn")
    has_prev = at > 0
    has_next = at < n_attn - 1

    high = rows - block
    top = rows - TQ
    tok_parts = [(top + TQ // 2, TQ // 2, 2), (top, TQ // 2, 1)]
    tok_parts += [(c, TQ, 6 + i) for i, c in enumerate(reversed(range(high, top, TQ)))]
    tok_parts += [(0, high, 2)] if high else []

    def tok_copy(i):
        start, size, slot = tok_parts[i]
        here = pl.ds(start, size)
        return pltpu.make_async_copy(tok.at[here], xt.at[here], own_sem.at[slot])

    weights = [
        (wk, lambda d: wkv_buf.at[d, :, pl.ds(0, kvw)]),
        (wv, lambda d: wkv_buf.at[d, :, pl.ds(kvw, kvw)]),
        (wq, lambda d: wq_buf.at[d]),
    ]

    def own_copy(i):
        src, dst = weights[i]
        return pltpu.make_async_copy(src, dst(0), own_sem.at[(3, 0, 5)[i]])

    def weight_copy(d, i):
        src, dst = weights[i]
        return pltpu.make_async_remote_copy(
            src_ref=src, dst_ref=dst(d),
            send_sem=w_send.at[d - 1, i], recv_sem=w_recv.at[d - 1, i],
            device_id={"rows": lax.rem(me + d, n_rows)}, device_id_type=MESH,
        )

    small = [
        pltpu.make_async_copy(src, dst, own_sem.at[i])
        for i, (src, dst) in enumerate(((gain_in, gain), (docs_in, docs)))
    ]
    tab_copy = pltpu.make_async_copy(
        table.at[pl.ds(pl.multiple_of(at * rows, rows), rows)], tab, own_sem.at[4]
    )

    small[0].start()
    tok_copy(0).start()
    tok_copy(1).start()
    own_copy(0).start()
    near = range(2, 2 + (top - high) // TQ)
    for i in near:
        tok_copy(i).start()
    tab_copy.start()

    barrier = pltpu.get_barrier_semaphore()
    paired = n_rows == 2 and n_attn > 1
    if paired:
        first = me == 0

        @pl.when(jnp.logical_not(first))
        def _():
            pl.semaphore_signal(barrier, inc=1, device_id={"rows": 0}, device_id_type=MESH)

        @pl.when(first)
        def _():
            pl.semaphore_wait(barrier, 1)
            pl.semaphore_signal(ready, inc=1, device_id={"rows": 1}, device_id_type=MESH)

        @pl.when(jnp.logical_not(first))
        def _():
            pl.semaphore_wait(ready, 1)
    else:
        for d in range(1, n_rows):
            pl.semaphore_signal(
                barrier, inc=1, device_id={"rows": lax.rem(me + d, n_rows)}, device_id_type=MESH
            )
        if back:

            @pl.when(has_prev)
            def _():
                pl.semaphore_signal(
                    barrier, inc=1, device_id={"attn": at - 1}, device_id_type=MESH
                )

            pl.semaphore_wait(barrier, n_rows - 1 + has_next.astype(jnp.int32))
        elif n_rows > 1:
            pl.semaphore_wait(barrier, n_rows - 1)

    for i in range(2):
        for d in range(1, n_rows):
            weight_copy(d, i).start()
    if paired:

        @pl.when(has_prev)
        def _():
            pl.semaphore_signal(
                barrier, inc=1, device_id={"rows": 1, "attn": at - 1}, device_id_type=MESH
            )

    for s in range(back):

        @pl.when(at - back + s < 0)
        def _():
            kbuf[pl.ds(s * rows, rows), :] = jnp.zeros((rows, kvw), BF16)
            vbuf[pl.ds(s * rows, rows), :] = jnp.zeros((rows, kvw), BF16)

    copies = hop_copies(rows, block, back)

    def hop(p):
        s, _, which, start, size = copies[p]
        ref = (kbuf, vbuf)[which]
        return pltpu.make_async_remote_copy(
            src_ref=ref.at[pl.ds((back - s) * rows + start, size)],
            dst_ref=ref.at[pl.ds((back - s - 1) * rows + start, size)],
            send_sem=kv_send.at[s], recv_sem=kv_recv.at[p],
            device_id={"attn": jnp.minimum(at + 1, n_attn - 1)}, device_id_type=MESH,
        )

    def all_sent(s):
        ref = kbuf.at[pl.ds(0, 2 * rows)]
        pltpu.make_async_remote_copy(
            src_ref=ref, dst_ref=ref, send_sem=kv_send.at[s], recv_sem=kv_recv.at[0],
            device_id={"attn": jnp.minimum(at + 1, n_attn - 1)}, device_id_type=MESH,
        ).wait_send()

    def send(which, start, size):
        if back:

            @pl.when(has_next)
            def _():
                for p, (s, _, kind, row, _) in enumerate(copies):
                    if s == 0 and kind == which and start <= row < start + size:
                        hop(p).start()

    def arrived(wanted):
        if wanted:

            @pl.when(at > copies[wanted[0]][0])
            def _():
                for p in wanted:
                    hop(p).wait_recv()

    def relay(count):
        for _ in range(min(count, len(relays))):
            s, unit = relays.pop(0)
            arrived([p for p, c in enumerate(copies) if c[:2] == (s, unit)])

            @pl.when((at > s) & has_next)
            def _():
                for p, c in enumerate(copies):
                    if c[:2] == (s + 1, unit):
                        hop(p).start()

    relays = [(s, unit) for s in range(back - 1) for unit in range(2 * (rows // block))]

    strip, piece = 16, 256

    def norm(start, size):
        @pl.loop(0, size // strip, unroll=4)
        def _(i):
            here = pl.ds(pl.multiple_of(start + i * strip, strip), strip)
            squares = jnp.zeros((strip, piece), F32)
            for k in range(width // piece):
                x = xt[here, pl.ds(k * piece, piece)].astype(F32)
                squares = squares + x * x
            mean_sq = jnp.sum(squares, axis=-1, keepdims=True) * (1.0 / width)
            scale = jnp.broadcast_to(lax.rsqrt(mean_sq + 1e-05), (strip, piece))
            for k in range(width // piece):
                cols = pl.ds(k * piece, piece)
                x = xt[here, cols].astype(F32) * scale
                xn[here, cols] = (
                    x.reshape(strip // 8, 8, piece) * gains[:, cols][None]
                ).reshape(strip, piece).astype(BF16)

    lane = lax.broadcasted_iota(jnp.int32, (1, HEAD), 1)

    def tables(start, size):
        t = tab[pl.ds(start, size), :]
        swapped = pltpu.roll(t, HEAD // 2, 1)
        low = lane < HEAD // 2
        return jnp.where(low, t, swapped), jnp.where(low, -swapped, t)

    def rotate(u, cosine, sine):
        return (u * cosine + pltpu.roll(u, HEAD // 2, 1) * sine).astype(BF16)

    half = depth // 2 if depth % (2 * HEAD) == 0 else depth

    def dots(start, size, terms, weight):
        total = None
        for d, k in terms:
            owner = lax.rem(me - d + n_rows, n_rows)
            here = pl.ds(pl.multiple_of(owner * depth + k, half), half)
            term = jnp.dot(
                xn[pl.ds(start, size), here], weight(d, k), preferred_element_type=F32
            )
            total = term if total is None else total + term
        return total

    def project(start, size, first_col, cols):
        def weight(d, k):
            return wkv_buf[d, pl.ds(k, half), pl.ds(first_col, cols)]

        terms = [(d, k) for d in range(n_rows) for k in range(0, depth, half)]
        for chain in range(2):
            sums[chain, pl.ds(0, size), pl.ds(0, cols)] = dots(
                start, size, terms[chain::2], weight
            )
        return sums[0, pl.ds(0, size), pl.ds(0, cols)] + sums[1, pl.ds(0, size), pl.ds(0, cols)]

    def store_keys(start, size, total):
        cosine, sine = tables(start, size)
        for h in range(kv_heads):
            cols = pl.ds(h * HEAD, HEAD)
            kbuf[pl.ds(mine + start, size), cols] = rotate(
                total[:, h * HEAD : (h + 1) * HEAD], cosine, sine
            )

    def store_values(start, size, total):
        vbuf[pl.ds(mine + start, size), :] = total.astype(BF16)

    def weight_ready(i):
        for d in range(1, n_rows):
            weight_copy(d, i).wait_recv()

    tok_copy(0).wait()
    small[0].wait()
    gains[...] = jnp.broadcast_to(gain[...].astype(F32).reshape(1, -1), gains.shape)
    norm(top + TQ // 2, TQ // 2)
    tok_copy(1).wait()
    norm(top, TQ // 2)
    own_copy(1).start()
    if high:
        tok_copy(len(tok_parts) - 1).start()
    for d in range(1, n_rows):
        weight_copy(d, 2).start()
    small[1].start()
    own_copy(2).start()

    key_cols = pl.ds(0, kvw)

    def key_weight(d, k):
        return wkv_buf[d, pl.ds(k, half), key_cols]

    own = [(0, k) for k in range(0, depth, half)]
    far = [(d, k) for d in range(1, n_rows) for k in range(0, depth, half)]
    here = pl.ds(0, TQ)
    own_copy(0).wait()
    for i in near:
        tok_copy(i).wait()
    for chain in range(2):
        sums[chain, here, key_cols] = (
            dots(top, TQ, own[chain::2], key_weight)
            if own[chain::2]
            else jnp.zeros((TQ, kvw), F32)
        )
    for i in near:
        norm(tok_parts[i][0], TQ)
    tab_copy.wait()
    weight_ready(0)
    for chain in range(2):
        if far[chain::2]:
            sums[chain, here, key_cols] = sums[chain, here, key_cols] + dots(
                top, TQ, far[chain::2], key_weight
            )
    store_keys(top, TQ, sums[0, here, key_cols] + sums[1, here, key_cols])
    if paired:

        @pl.when(has_next & jnp.logical_not(first))
        def _():
            pl.semaphore_wait(barrier, 2)
            pl.semaphore_signal(ready, inc=1, device_id={"rows": 0}, device_id_type=MESH)

        @pl.when(has_next & first)
        def _():
            pl.semaphore_wait(ready, 1)

    send(0, top, TQ)
    for i in near:
        start = tok_parts[i][0]
        store_keys(start, TQ, project(start, TQ, 0, kvw))
        send(0, start, TQ)
    own_copy(1).wait()
    weight_ready(1)
    store_values(high, block, project(high, block, kvw, kvw))
    send(1, high, block)
    if high:
        tok_copy(len(tok_parts) - 1).wait()
        norm(0, high)
    for b in reversed(range(high // block)):
        store_keys(b * block, block, project(b * block, block, 0, kvw))
        send(0, b * block, block)
        store_values(b * block, block, project(b * block, block, kvw, kvw))
        send(1, b * block, block)
    small[1].wait()
    for s in range(back + 1):
        owner = at - back + s
        keep = pl.multiple_of(jnp.maximum(owner, 0) * rows, rows)
        kdoc[:, pl.ds(s * rows, rows)] = jnp.where(owner >= 0, docs[:, pl.ds(keep, rows)], -1)
    for t in range(tiles):
        row = kdoc[:, pl.ds(mine + t * TQ, TQ)]
        qdoc[pl.ds(t * TQ, TQ), :] = jnp.broadcast_to(row, (TQ, TQ)).T

    def queries(start, d):
        owner = lax.rem(me - d + n_rows, n_rows)
        here = pl.ds(pl.multiple_of(owner * depth, depth), depth)
        return jnp.dot(xn[pl.ds(start, block), here], wq_buf[d], preferred_element_type=F32)

    steps = [b * block for b in reversed(range(rows // block))]
    own_copy(2).wait()
    for start in steps:
        qsum[pl.ds(start, block), :] = queries(start, 0)
    relay(1)
    for d in range(1, n_rows):
        weight_copy(d, 2).wait_recv()
    for start in steps:
        total = qsum[pl.ds(start, block), :]
        for d in range(1, n_rows):
            total = total + queries(start, d)
        cosine, sine = tables(start, block)
        for h in range(kv_heads):
            for g in range(group):
                col = (h * group + g) * HEAD
                u = rotate(total[:, col : col + HEAD], cosine, sine)
                for t in range(block // TQ):
                    q[start // TQ + t, h, pl.ds(g * TQ, TQ), :] = u[t * TQ : (t + 1) * TQ]
    relay(1)

    factor = math.log2(math.e) / math.sqrt(HEAD)

    def weigh(t, s, lo, size, opens):
        seen = s * rows + lo
        keys_at = pl.ds(seen, size)
        visible = jnp.tile(qdoc[pl.ds(t * TQ, TQ), :], (1, size // TQ)) == kdoc[:, keys_at]
        if s == back:
            query_at = lax.broadcasted_iota(jnp.int32, (TQ, 1), 0) + t * TQ
            key_at = lax.broadcasted_iota(jnp.int32, (1, size), 1) + lo
            visible = visible & (query_at >= key_at)
        made = []
        for h in range(kv_heads):
            scores = lax.dot_general(
                q[t, h], kbuf[keys_at, pl.ds(h * HEAD, HEAD)], (((1,), (1,)), ((), ())),
                preferred_element_type=F32,
            )
            scores = jnp.where(
                visible[None], scores.reshape(group, TQ, size), -1e30
            ).reshape(group * TQ, size)
            top = jnp.broadcast_to(
                jnp.max(scores, axis=-1, keepdims=True), (group * TQ, HEAD)
            )
            fade = None
            if not opens:
                older = tops[t, h]
                top = jnp.maximum(older, top)
                fade = jnp.exp2((older - top) * factor)
            weight = jnp.exp2((scores - jnp.tile(top, (1, size // HEAD))) * factor).astype(BF16)
            made.append((weight, fade))
            tops[t, h] = top
        return made

    def mix(t, s, lo, size, made, closes):
        keys_at = pl.ds(s * rows + lo, size)
        for h in range(kv_heads):
            weight, fade = made[h]
            mixed = jnp.dot(
                weight,
                jnp.concatenate(
                    [vbuf[keys_at, pl.ds(h * HEAD, HEAD)], jnp.ones((size, HEAD), BF16)], axis=1
                ),
                preferred_element_type=F32,
            )
            if fade is not None:
                mixed = acc[t, h] * jnp.tile(fade, (1, 2)) + mixed
            if closes:
                done = (mixed[:, :HEAD] / mixed[:, HEAD:]).astype(BF16)
                for g in range(group):
                    out[pl.ds(t * TQ, TQ), pl.ds((h * group + g) * HEAD, HEAD)] = done[
                        g * TQ : (g + 1) * TQ
                    ]
            else:
                acc[t, h] = mixed

    def attend(t, s, lo, size, opens, closes):
        mix(t, s, lo, size, weigh(t, s, lo, size, opens), closes)

    def reach(t, s):
        return max(mine + (t + 1) * TQ - span - s * rows, 0)

    def final(t, s, lo):
        return lo <= reach(t, s) and all(reach(t, b) >= rows for b in range(s))

    for i, t in enumerate(reversed(range(tiles))):
        lo = reach(t, back)
        attend(t, back, lo, (t + 1) * TQ - lo, True, final(t, back, lo))
        if i % 2:
            relay(1)
    relay(len(relays))
    for s in reversed(range(1, back)):
        for t in reversed(range(tiles)):
            lo = reach(t, s)
            if lo < rows:
                attend(t, s, lo, rows - lo, False, final(t, s, lo))
    for i in range(len(weights)):
        for d in range(1, n_rows):
            weight_copy(d, i).wait_send()
    def come(which, start, size):
        arrived([
            p
            for p, (s, _, kind, row, length) in enumerate(copies)
            if s == back - 1 and kind == which and start < row + length <= start + size
        ])

    def sent_all():
        for s in range(back):

            @pl.when((at >= s) & has_next)
            def _():
                all_sent(s)

    blocks = list(reversed(range(0, rows, block))) if back else []
    for start in blocks:
        end = start + block
        low = {t: max(reach(t, 0), start) for t in reversed(range(tiles))}
        low = {t: lo for t, lo in low.items() if lo < end}
        if start == high and start > 0:
            come(0, start, block)
            made = {t: weigh(t, 0, lo, end - lo, False) for t, lo in low.items()}
            come(1, start, block)
            for t, lo in low.items():
                mix(t, 0, lo, end - lo, made[t], final(t, 0, lo))
            continue
        pairs = [(t, h) for t in low for h in range(kv_heads)]
        base = {(t, h): acc[t, h][:, :HEAD] for t, h in pairs}
        total = {(t, h): acc[t, h][:, HEAD:] for t, h in pairs}
        made = {}
        for c in reversed(range(start, end, TQ)):
            come(0, c, TQ)
            for t, lo in low.items():
                if lo > c:
                    continue
                for h, (weight, fade) in enumerate(weigh(t, 0, c, TQ, False)):
                    for e in range(c + TQ, end, TQ):
                        older, carry = made[t, h, e]
                        made[t, h, e] = older, fade if carry is None else carry * fade
                    made[t, h, c] = weight, None
                    base[t, h] = base[t, h] * fade
                    total[t, h] = total[t, h] * fade + jnp.dot(
                        weight, jnp.ones((TQ, HEAD), BF16), preferred_element_type=F32
                    )
                    if c == lo and final(t, 0, lo):
                        total[t, h] = 1.0 / total[t, h]
        for c in reversed(range(start, end, TQ)):
            if c == 0:
                sent_all()
            come(1, c, TQ)
            for t, h in pairs:
                if low[t] > c:
                    continue
                weight, carry = made[t, h, c]
                fresh = jnp.dot(
                    weight, vbuf[pl.ds(c, TQ), pl.ds(h * HEAD, HEAD)],
                    preferred_element_type=F32,
                )
                base[t, h] = base[t, h] + (fresh if carry is None else fresh * carry)
                if low[t] < c:
                    continue
                if final(t, 0, low[t]):
                    done = (base[t, h] * total[t, h]).astype(BF16)
                    for g in range(group):
                        out[pl.ds(t * TQ, TQ), pl.ds((h * group + g) * HEAD, HEAD)] = done[
                            g * TQ : (g + 1) * TQ
                        ]
                else:
                    acc[t, h] = jnp.concatenate([base[t, h], total[t, h]], axis=1)


def solution(mesh):
    n_rows = mesh.shape["rows"]
    n_attn = mesh.shape["attn"]

    def on_device(tokens, norm_gain, w_query, w_key, w_value, documents):
        rows, width = tokens.shape
        depth, qw = w_query.shape
        kvw = w_key.shape[1]
        back = min(n_attn - 1, -(-(MOST - 1) // rows))
        block = 2 * TQ if rows % (2 * TQ) == 0 else rows
        hops = len(hop_copies(rows, block, back))
        near = (block - TQ) // TQ
        table = jnp.asarray(rotary_table(documents.shape[1]))
        hbm = pl.BlockSpec(memory_space=pl.ANY)
        vmem = pl.BlockSpec(memory_space=pltpu.VMEM)
        keys = (back + 1) * rows
        group = qw // kvw
        heads = kvw // HEAD
        tiles = rows // TQ
        args = (tokens, norm_gain, w_query, w_key, w_value, documents, table)
        return pl.pallas_call(
            functools.partial(kernel, n_rows, n_attn, back, block),
            out_shape=pltpu.VMEM((rows, qw), BF16),
            in_specs=[hbm] * len(args),
            out_specs=vmem,
            scratch_shapes=[
                pltpu.VMEM((width,), BF16),
                pltpu.VMEM(documents.shape, jnp.int32),
                pltpu.VMEM((8, width), F32),
                pltpu.VMEM((rows, width), BF16),
                pltpu.VMEM((rows, width), BF16),
                pltpu.VMEM((n_rows, depth, 2 * kvw), BF16),
                pltpu.VMEM((n_rows, depth, qw), BF16),
                pltpu.VMEM((keys, kvw), BF16),
                pltpu.VMEM((keys, kvw), BF16),
                pltpu.VMEM((tiles, heads, group * TQ, HEAD), BF16),
                pltpu.VMEM((tiles, heads, group * TQ, HEAD), F32),
                pltpu.VMEM((tiles, heads, group * TQ, 2 * HEAD), F32),
                pltpu.VMEM((2, block, 2 * kvw), F32),
                pltpu.VMEM((rows, qw), F32),
                pltpu.VMEM((rows, HEAD), F32),
                pltpu.VMEM((1, keys), jnp.int32),
                pltpu.VMEM((rows, TQ), jnp.int32),
                pltpu.SemaphoreType.DMA((6 + near,)),
                pltpu.SemaphoreType.DMA((max(n_rows - 1, 1), 3)),
                pltpu.SemaphoreType.DMA((max(n_rows - 1, 1), 3)),
                pltpu.SemaphoreType.DMA((max(back, 1),)),
                pltpu.SemaphoreType.DMA((max(hops, 1),)),
                pltpu.SemaphoreType.REGULAR,
            ],
            compiler_params=pltpu.CompilerParams(
                collective_id=0, has_side_effects=True, vmem_limit_bytes=48 << 20
            ),
            name="layer",
        )(*(pltpu.with_memory_space_constraint(a, pltpu.HBM) for a in args))

    placed = (
        P(("rows", "attn"), None),
        P(),
        P("rows", "tp"),
        P("rows", "tp"),
        P("rows", "tp"),
        P("rows", None),
    )
    return jax.shard_map(
        on_device, mesh=mesh, in_specs=placed, out_specs=P(("rows", "attn"), "tp"), check_vma=False
    )
```

```python
import functools
import math

import jax
import jax.numpy as jnp
import numpy as np
from jax import lax
from jax.experimental import pallas as pl
from jax.experimental.pallas import tpu as pltpu
from jax.sharding import PartitionSpec as P

HEAD = 128
MOST = 1024
TQ = 128
BF16 = jnp.bfloat16
F32 = jnp.float32
MESH = pl.DeviceIdType.MESH


def rotary_table(window):
    half = HEAD // 2
    frequency = np.exp(
        np.arange(half, dtype=np.float32) * np.float32(-2.0 * math.log(500000.0) / HEAD)
    ).astype(np.float32)
    angles = np.arange(window, dtype=np.float32)[:, None] * frequency[None, :]
    return np.concatenate([np.cos(angles), np.sin(angles)], axis=1).astype(np.float32)


def hop_copies(rows, block, back):
    copies = []
    for s in range(back):
        unit = 0
        for b in reversed(range(rows // block)):
            for which in range(2):
                upper = b == rows // block - 1
                fine = (upper and which == 0) if s == 0 else (s == back - 1 and not upper)
                size = TQ if fine else block
                for start in reversed(range(b * block, (b + 1) * block, size)):
                    copies.append((s, unit, which, start, size))
                unit += 1
    return copies


def kernel(
    n_rows, n_attn, back, block,
    tok, gain_in, wq, wk, wv, docs_in, table, out,
    gain, docs, gains, xt, xn, wkv_buf, wq_buf, kbuf, vbuf, q, tops, acc, sums, qsum, tab, kdoc, qdoc, kmask,
    own_sem, w_send, w_recv, kv_send, kv_recv, ready,
):
    rows, width = tok.shape
    depth, kvw = wk.shape
    qw = wq.shape[1]
    kv_heads = kvw // HEAD
    group = qw // kvw
    tiles = rows // TQ
    mine = back * rows
    span = min(mine + rows, -(-(MOST - 1 + TQ) // TQ) * TQ)
    me = lax.axis_index("rows")
    at = lax.axis_index("attn")
    has_prev = at > 0
    has_next = at < n_attn - 1

    high = rows - block
    top = rows - TQ
    tok_parts = [(top + TQ // 2, TQ // 2, 2), (top, TQ // 2, 1)]
    tok_parts += [(c, TQ, 6 + i) for i, c in enumerate(reversed(range(high, top, TQ)))]
    tok_parts += [(0, high, 2)] if high else []

    def tok_copy(i):
        start, size, slot = tok_parts[i]
        here = pl.ds(start, size)
        return pltpu.make_async_copy(tok.at[here], xt.at[here], own_sem.at[slot])

    weights = [
        (wk, lambda d: wkv_buf.at[d, :, pl.ds(0, kvw)]),
        (wv, lambda d: wkv_buf.at[d, :, pl.ds(kvw, kvw)]),
        (wq, lambda d: wq_buf.at[d]),
    ]

    def own_copy(i):
        src, dst = weights[i]
        return pltpu.make_async_copy(src, dst(0), own_sem.at[(3, 0, 5)[i]])

    def weight_copy(d, i):
        src, dst = weights[i]
        return pltpu.make_async_remote_copy(
            src_ref=src, dst_ref=dst(d),
            send_sem=w_send.at[d - 1, i], recv_sem=w_recv.at[d - 1, i],
            device_id={"rows": lax.rem(me + d, n_rows)}, device_id_type=MESH,
        )

    small = [
        pltpu.make_async_copy(src, dst, own_sem.at[i])
        for i, (src, dst) in enumerate(((gain_in, gain), (docs_in, docs)))
    ]
    tab_copy = pltpu.make_async_copy(
        table.at[pl.ds(pl.multiple_of(at * rows, rows), rows)], tab, own_sem.at[4]
    )

    small[0].start()
    tok_copy(0).start()
    tok_copy(1).start()
    own_copy(0).start()
    near = range(2, 2 + (top - high) // TQ)
    for i in near:
        tok_copy(i).start()
    tab_copy.start()

    barrier = pltpu.get_barrier_semaphore()
    paired = n_rows == 2 and n_attn > 1
    if paired:
        first = me == 0

        @pl.when(jnp.logical_not(first))
        def _():
            pl.semaphore_signal(barrier, inc=1, device_id={"rows": 0}, device_id_type=MESH)

        @pl.when(first)
        def _():
            pl.semaphore_wait(barrier, 1)
            pl.semaphore_signal(ready, inc=1, device_id={"rows": 1}, device_id_type=MESH)

        @pl.when(jnp.logical_not(first))
        def _():
            pl.semaphore_wait(ready, 1)
    else:
        for d in range(1, n_rows):
            pl.semaphore_signal(
                barrier, inc=1, device_id={"rows": lax.rem(me + d, n_rows)}, device_id_type=MESH
            )
        if back:

            @pl.when(has_prev)
            def _():
                pl.semaphore_signal(
                    barrier, inc=1, device_id={"attn": at - 1}, device_id_type=MESH
                )

            pl.semaphore_wait(barrier, n_rows - 1 + has_next.astype(jnp.int32))
        elif n_rows > 1:
            pl.semaphore_wait(barrier, n_rows - 1)

    for i in range(2):
        for d in range(1, n_rows):
            weight_copy(d, i).start()
    if paired:

        @pl.when(has_prev)
        def _():
            pl.semaphore_signal(
                barrier, inc=1, device_id={"rows": 1, "attn": at - 1}, device_id_type=MESH
            )

    for s in range(back):

        @pl.when(at - back + s < 0)
        def _():
            kbuf[pl.ds(s * rows, rows), :] = jnp.zeros((rows, kvw), BF16)
            vbuf[pl.ds(s * rows, rows), :] = jnp.zeros((rows, kvw), BF16)

    copies = hop_copies(rows, block, back)

    def hop(p):
        s, _, which, start, size = copies[p]
        ref = (kbuf, vbuf)[which]
        return pltpu.make_async_remote_copy(
            src_ref=ref.at[pl.ds((back - s) * rows + start, size)],
            dst_ref=ref.at[pl.ds((back - s - 1) * rows + start, size)],
            send_sem=kv_send.at[s], recv_sem=kv_recv.at[p],
            device_id={"attn": jnp.minimum(at + 1, n_attn - 1)}, device_id_type=MESH,
        )

    def all_sent(s):
        ref = kbuf.at[pl.ds(0, 2 * rows)]
        pltpu.make_async_remote_copy(
            src_ref=ref, dst_ref=ref, send_sem=kv_send.at[s], recv_sem=kv_recv.at[0],
            device_id={"attn": jnp.minimum(at + 1, n_attn - 1)}, device_id_type=MESH,
        ).wait_send()

    def send(which, start, size):
        if back:

            @pl.when(has_next)
            def _():
                for p, (s, _, kind, row, _) in enumerate(copies):
                    if s == 0 and kind == which and start <= row < start + size:
                        hop(p).start()

    def arrived(wanted):
        if wanted:

            @pl.when(at > copies[wanted[0]][0])
            def _():
                for p in wanted:
                    hop(p).wait_recv()

    def relay(count):
        for _ in range(min(count, len(relays))):
            s, unit = relays.pop(0)
            arrived([p for p, c in enumerate(copies) if c[:2] == (s, unit)])

            @pl.when((at > s) & has_next)
            def _():
                for p, c in enumerate(copies):
                    if c[:2] == (s + 1, unit):
                        hop(p).start()

    relays = [(s, unit) for s in range(back - 1) for unit in range(2 * (rows // block))]

    strip, piece = 16, 256

    def norm(start, size):
        for first_row in reversed(range(start, start + size, 4 * strip)):
            norm_rows(first_row)

    def norm_rows(start):
        @pl.loop(0, 4, unroll=4)
        def _(i):
            here = pl.ds(pl.multiple_of(start + i * strip, strip), strip)
            squares = jnp.zeros((strip, piece), F32)
            for k in range(width // piece):
                x = xt[here, pl.ds(k * piece, piece)].astype(F32)
                squares = squares + x * x
            mean_sq = jnp.sum(squares, axis=-1, keepdims=True) * (1.0 / width)
            scale = jnp.broadcast_to(lax.rsqrt(mean_sq + 1e-05), (strip, piece))
            for k in range(width // piece):
                cols = pl.ds(k * piece, piece)
                x = xt[here, cols].astype(F32) * scale
                xn[here, cols] = (
                    x.reshape(strip // 8, 8, piece) * gains[:, cols][None]
                ).reshape(strip, piece).astype(BF16)

    lane = lax.broadcasted_iota(jnp.int32, (1, HEAD), 1)

    def tables(start, size):
        t = tab[pl.ds(start, size), :]
        swapped = pltpu.roll(t, HEAD // 2, 1)
        low = lane < HEAD // 2
        return jnp.where(low, t, swapped), jnp.where(low, -swapped, t)

    def rotate(u, cosine, sine):
        return (u * cosine + pltpu.roll(u, HEAD // 2, 1) * sine).astype(BF16)

    half = depth // 2 if depth % (2 * HEAD) == 0 else depth

    def dots(start, size, terms, weight):
        total = None
        for d, k in terms:
            owner = lax.rem(me - d + n_rows, n_rows)
            here = pl.ds(pl.multiple_of(owner * depth + k, half), half)
            term = jnp.dot(
                xn[pl.ds(start, size), here], weight(d, k), preferred_element_type=F32
            )
            total = term if total is None else total + term
        return total

    def project(start, size, first_col, cols):
        def weight(d, k):
            return wkv_buf[d, pl.ds(k, half), pl.ds(first_col, cols)]

        terms = [(d, k) for d in range(n_rows) for k in range(0, depth, half)]
        for chain in range(2):
            sums[chain, pl.ds(0, size), pl.ds(0, cols)] = dots(
                start, size, terms[chain::2], weight
            )
        return sums[0, pl.ds(0, size), pl.ds(0, cols)] + sums[1, pl.ds(0, size), pl.ds(0, cols)]

    def store_keys(start, size, total):
        cosine, sine = tables(start, size)
        for h in range(kv_heads):
            cols = pl.ds(h * HEAD, HEAD)
            kbuf[pl.ds(mine + start, size), cols] = rotate(
                total[:, h * HEAD : (h + 1) * HEAD], cosine, sine
            )

    def store_values(start, size, total):
        vbuf[pl.ds(mine + start, size), :] = total.astype(BF16)

    def weight_ready(i):
        for d in range(1, n_rows):
            weight_copy(d, i).wait_recv()

    tok_copy(0).wait()
    small[0].wait()
    gains[...] = jnp.broadcast_to(gain[...].astype(F32).reshape(1, -1), gains.shape)
    norm(top + TQ // 2, TQ // 2)
    tok_copy(1).wait()
    norm(top, TQ // 2)
    own_copy(1).start()
    if high:
        tok_copy(len(tok_parts) - 1).start()
    for d in range(1, n_rows):
        weight_copy(d, 2).start()
    small[1].start()
    own_copy(2).start()

    key_cols = pl.ds(0, kvw)

    def key_weight(d, k):
        return wkv_buf[d, pl.ds(k, half), key_cols]

    own = [(0, k) for k in range(0, depth, half)]
    far = [(d, k) for d in range(1, n_rows) for k in range(0, depth, half)]
    here = pl.ds(0, TQ)
    own_copy(0).wait()
    for i in near:
        tok_copy(i).wait()
    for chain in range(2):
        sums[chain, here, key_cols] = (
            dots(top, TQ, own[chain::2], key_weight)
            if own[chain::2]
            else jnp.zeros((TQ, kvw), F32)
        )
    for i in near:
        norm(tok_parts[i][0], TQ)
    tab_copy.wait()
    weight_ready(0)
    for chain in range(2):
        if far[chain::2]:
            sums[chain, here, key_cols] = sums[chain, here, key_cols] + dots(
                top, TQ, far[chain::2], key_weight
            )
    store_keys(top, TQ, sums[0, here, key_cols] + sums[1, here, key_cols])
    if paired:

        @pl.when(has_next & jnp.logical_not(first))
        def _():
            pl.semaphore_wait(barrier, 2)
            pl.semaphore_signal(ready, inc=1, device_id={"rows": 0}, device_id_type=MESH)

        @pl.when(has_next & first)
        def _():
            pl.semaphore_wait(ready, 1)

    send(0, top, TQ)
    for i in near:
        start = tok_parts[i][0]
        store_keys(start, TQ, project(start, TQ, 0, kvw))
        send(0, start, TQ)
    own_copy(1).wait()
    weight_ready(1)
    store_values(high, block, project(high, block, kvw, kvw))
    send(1, high, block)
    if high:
        tok_copy(len(tok_parts) - 1).wait()
        norm(0, high)
    for b in reversed(range(high // block)):
        store_keys(b * block, block, project(b * block, block, 0, kvw))
        send(0, b * block, block)
        store_values(b * block, block, project(b * block, block, kvw, kvw))
        send(1, b * block, block)
    small[1].wait()
    for s in range(back + 1):
        owner = at - back + s
        keep = pl.multiple_of(jnp.maximum(owner, 0) * rows, rows)
        kdoc[:, pl.ds(s * rows, rows)] = jnp.where(owner >= 0, docs[:, pl.ds(keep, rows)], -1)
    lanes = lax.broadcasted_iota(jnp.int32, (TQ, HEAD), 1)
    for k in range((back + 1) * tiles):
        here = pl.ds(k * TQ, TQ)
        column = jnp.broadcast_to(kdoc[:, here], (HEAD, TQ)).T
        same = column == lanes
        kmask[here, :] = jnp.where(same, 0.0, -1e30).astype(BF16)
        if k >= back * tiles:
            qdoc[pl.ds((k - back * tiles) * TQ, TQ), :] = column
            chosen = jnp.where(same, 1.0, 0.0).astype(BF16)
            for h in range(kv_heads):
                for g in range(group):
                    q[k - back * tiles, h, pl.ds(g * TQ, TQ), pl.ds(HEAD, HEAD)] = chosen

    def queries(start, d):
        owner = lax.rem(me - d + n_rows, n_rows)
        here = pl.ds(pl.multiple_of(owner * depth, depth), depth)
        return jnp.dot(xn[pl.ds(start, block), here], wq_buf[d], preferred_element_type=F32)

    steps = [b * block for b in reversed(range(rows // block))]
    own_copy(2).wait()
    for start in steps:
        qsum[pl.ds(start, block), :] = queries(start, 0)
    relay(1)
    for d in range(1, n_rows):
        weight_copy(d, 2).wait_recv()
    for start in steps:
        total = qsum[pl.ds(start, block), :]
        for d in range(1, n_rows):
            total = total + queries(start, d)
        cosine, sine = tables(start, block)
        for h in range(kv_heads):
            for g in range(group):
                col = (h * group + g) * HEAD
                u = rotate(total[:, col : col + HEAD], cosine, sine)
                for t in range(block // TQ):
                    q[start // TQ + t, h, pl.ds(g * TQ, TQ), pl.ds(0, HEAD)] = u[t * TQ : (t + 1) * TQ]
    relay(1)

    factor = math.log2(math.e) / math.sqrt(HEAD)

    def weigh(t, s, lo, size, opens):
        keys_at = pl.ds(s * rows + lo, size)
        made = []
        for h in range(kv_heads):
            keys = kbuf[keys_at, pl.ds(h * HEAD, HEAD)]
            small = s == 0 and size == TQ
            asked = q[t, h, :, pl.ds(0, HEAD)] if small else q[t, h]
            scores = lax.dot_general(
                asked,
                keys if small else jnp.concatenate([keys, kmask[keys_at, :]], axis=1),
                (((1,), (1,)), ((), ())),
                preferred_element_type=F32,
            )
            if small:
                seen = qdoc[pl.ds(t * TQ, TQ), :] == kdoc[:, keys_at]
                scores = jnp.where(
                    seen[None], scores.reshape(group, TQ, TQ), -1e30
                ).reshape(group * TQ, TQ)
            if s == back:
                ahead = lanes > lax.broadcasted_iota(jnp.int32, (TQ, HEAD), 0)
                edge = scores[:, size - TQ :].reshape(group, TQ, TQ)
                edge = jnp.where(ahead[None], -1e30, edge).reshape(group * TQ, TQ)
                scores = (
                    edge
                    if size == TQ
                    else jnp.concatenate([scores[:, : size - TQ], edge], axis=1)
                )
            top = jnp.broadcast_to(
                jnp.max(scores, axis=-1, keepdims=True), (group * TQ, HEAD)
            )
            fade = None
            if not opens:
                older = tops[t, h]
                top = jnp.maximum(older, top)
                fade = jnp.exp2((older - top) * factor)
            weight = jnp.exp2((scores - jnp.tile(top, (1, size // HEAD))) * factor).astype(BF16)
            made.append((weight, fade))
            tops[t, h] = top
        return made

    def mix(t, s, lo, size, made, closes):
        keys_at = pl.ds(s * rows + lo, size)
        for h in range(kv_heads):
            weight, fade = made[h]
            mixed = jnp.dot(
                weight,
                jnp.concatenate(
                    [vbuf[keys_at, pl.ds(h * HEAD, HEAD)], jnp.ones((size, HEAD), BF16)], axis=1
                ),
                preferred_element_type=F32,
            )
            if fade is not None:
                mixed = acc[t, h] * jnp.tile(fade, (1, 2)) + mixed
            if closes:
                done = (mixed[:, :HEAD] / mixed[:, HEAD:]).astype(BF16)
                for g in range(group):
                    out[pl.ds(t * TQ, TQ), pl.ds((h * group + g) * HEAD, HEAD)] = done[
                        g * TQ : (g + 1) * TQ
                    ]
            else:
                acc[t, h] = mixed

    def attend(t, s, lo, size, opens, closes):
        mix(t, s, lo, size, weigh(t, s, lo, size, opens), closes)

    def reach(t, s):
        return max(mine + (t + 1) * TQ - span - s * rows, 0)

    def final(t, s, lo):
        return lo <= reach(t, s) and all(reach(t, b) >= rows for b in range(s))

    for i, t in enumerate(reversed(range(tiles))):
        lo = reach(t, back)
        attend(t, back, lo, (t + 1) * TQ - lo, True, final(t, back, lo))
        if i % 2:
            relay(1)
    relay(len(relays))
    for s in reversed(range(1, back)):
        for t in reversed(range(tiles)):
            lo = reach(t, s)
            if lo < rows:
                attend(t, s, lo, rows - lo, False, final(t, s, lo))
    for i in range(len(weights)):
        for d in range(1, n_rows):
            weight_copy(d, i).wait_send()
    def come(which, start, size):
        arrived([
            p
            for p, (s, _, kind, row, length) in enumerate(copies)
            if s == back - 1 and kind == which and start < row + length <= start + size
        ])

    def sent_all():
        for s in range(back):

            @pl.when((at >= s) & has_next)
            def _():
                all_sent(s)

    blocks = list(reversed(range(0, rows, block))) if back else []
    for start in blocks:
        end = start + block
        low = {t: max(reach(t, 0), start) for t in reversed(range(tiles))}
        low = {t: lo for t, lo in low.items() if lo < end}
        if start == high and start > 0:
            come(0, start, block)
            made = {t: weigh(t, 0, lo, end - lo, False) for t, lo in low.items()}
            come(1, start, block)
            for t, lo in low.items():
                mix(t, 0, lo, end - lo, made[t], final(t, 0, lo))
            continue
        pairs = [(t, h) for t in low for h in range(kv_heads)]
        base = {(t, h): acc[t, h][:, :HEAD] for t, h in pairs}
        total = {(t, h): acc[t, h][:, HEAD:] for t, h in pairs}
        made = {}
        for c in reversed(range(start, end, TQ)):
            come(0, c, TQ)
            for t, lo in low.items():
                if lo > c:
                    continue
                for h, (weight, fade) in enumerate(weigh(t, 0, c, TQ, False)):
                    for e in range(c + TQ, end, TQ):
                        older, carry = made[t, h, e]
                        made[t, h, e] = older, fade if carry is None else carry * fade
                    made[t, h, c] = weight, None
                    base[t, h] = base[t, h] * fade
                    total[t, h] = total[t, h] * fade + jnp.dot(
                        weight, jnp.ones((TQ, HEAD), BF16), preferred_element_type=F32
                    )
                    if c == lo and final(t, 0, lo):
                        total[t, h] = 1.0 / total[t, h]
        for c in reversed(range(start, end, TQ)):
            if c == 0:
                sent_all()
            come(1, c, TQ)
            for t, h in pairs:
                if low[t] > c:
                    continue
                weight, carry = made[t, h, c]
                fresh = jnp.dot(
                    weight, vbuf[pl.ds(c, TQ), pl.ds(h * HEAD, HEAD)],
                    preferred_element_type=F32,
                )
                base[t, h] = base[t, h] + (fresh if carry is None else fresh * carry)
                if low[t] < c:
                    continue
                if final(t, 0, low[t]):
                    done = (base[t, h] * total[t, h]).astype(BF16)
                    for g in range(group):
                        out[pl.ds(t * TQ, TQ), pl.ds((h * group + g) * HEAD, HEAD)] = done[
                            g * TQ : (g + 1) * TQ
                        ]
                else:
                    acc[t, h] = jnp.concatenate([base[t, h], total[t, h]], axis=1)


def solution(mesh):
    n_rows = mesh.shape["rows"]
    n_attn = mesh.shape["attn"]

    def on_device(tokens, norm_gain, w_query, w_key, w_value, documents):
        rows, width = tokens.shape
        depth, qw = w_query.shape
        kvw = w_key.shape[1]
        back = min(n_attn - 1, -(-(MOST - 1) // rows))
        block = 2 * TQ if rows % (2 * TQ) == 0 else rows
        hops = len(hop_copies(rows, block, back))
        near = (block - TQ) // TQ
        table = jnp.asarray(rotary_table(documents.shape[1]))
        hbm = pl.BlockSpec(memory_space=pl.ANY)
        vmem = pl.BlockSpec(memory_space=pltpu.VMEM)
        keys = (back + 1) * rows
        group = qw // kvw
        heads = kvw // HEAD
        tiles = rows // TQ
        args = (tokens, norm_gain, w_query, w_key, w_value, documents, table)
        return pl.pallas_call(
            functools.partial(kernel, n_rows, n_attn, back, block),
            out_shape=pltpu.VMEM((rows, qw), BF16),
            in_specs=[hbm] * len(args),
            out_specs=vmem,
            scratch_shapes=[
                pltpu.VMEM((width,), BF16),
                pltpu.VMEM(documents.shape, jnp.int32),
                pltpu.VMEM((8, width), F32),
                pltpu.VMEM((rows, width), BF16),
                pltpu.VMEM((rows, width), BF16),
                pltpu.VMEM((n_rows, depth, 2 * kvw), BF16),
                pltpu.VMEM((n_rows, depth, qw), BF16),
                pltpu.VMEM((keys, kvw), BF16),
                pltpu.VMEM((keys, kvw), BF16),
                pltpu.VMEM((tiles, heads, group * TQ, 2 * HEAD), BF16),
                pltpu.VMEM((tiles, heads, group * TQ, HEAD), F32),
                pltpu.VMEM((tiles, heads, group * TQ, 2 * HEAD), F32),
                pltpu.VMEM((2, block, 2 * kvw), F32),
                pltpu.VMEM((rows, qw), F32),
                pltpu.VMEM((rows, HEAD), F32),
                pltpu.VMEM((1, keys), jnp.int32),
                pltpu.VMEM((rows, HEAD), jnp.int32),
                pltpu.VMEM((keys, HEAD), BF16),
                pltpu.SemaphoreType.DMA((6 + near,)),
                pltpu.SemaphoreType.DMA((max(n_rows - 1, 1), 3)),
                pltpu.SemaphoreType.DMA((max(n_rows - 1, 1), 3)),
                pltpu.SemaphoreType.DMA((max(back, 1),)),
                pltpu.SemaphoreType.DMA((max(hops, 1),)),
                pltpu.SemaphoreType.REGULAR,
            ],
            compiler_params=pltpu.CompilerParams(
                collective_id=0, has_side_effects=True, vmem_limit_bytes=48 << 20
            ),
            name="layer",
        )(*(pltpu.with_memory_space_constraint(a, pltpu.HBM) for a in args))

    placed = (
        P(("rows", "attn"), None),
        P(),
        P("rows", "tp"),
        P("rows", "tp"),
        P("rows", "tp"),
        P("rows", None),
    )
    return jax.shard_map(
        on_device, mesh=mesh, in_specs=placed, out_specs=P(("rows", "attn"), "tp"), check_vma=False
    )
```

```python
import functools
import math

import jax
import jax.numpy as jnp
import numpy as np
from jax import lax
from jax.experimental import pallas as pl
from jax.experimental.pallas import tpu as pltpu
from jax.sharding import PartitionSpec as P

HEAD = 128
MOST = 1024
TQ = 128
BF16 = jnp.bfloat16
F32 = jnp.float32
MESH = pl.DeviceIdType.MESH


def rotary_table(window):
    half = HEAD // 2
    frequency = np.exp(
        np.arange(half, dtype=np.float32) * np.float32(-2.0 * math.log(500000.0) / HEAD)
    ).astype(np.float32)
    angles = np.arange(window, dtype=np.float32)[:, None] * frequency[None, :]
    return np.concatenate([np.cos(angles), np.sin(angles)], axis=1).astype(np.float32)


def hop_copies(rows, block, back):
    copies = []
    for s in range(back):
        unit = 0
        for b in reversed(range(rows // block)):
            for which in range(2):
                upper = b == rows // block - 1
                fine = (upper and which == 0) if s == 0 else (s == back - 1 and not upper)
                size = TQ if fine else block
                for start in reversed(range(b * block, (b + 1) * block, size)):
                    copies.append((s, unit, which, start, size))
                unit += 1
    return copies


def kernel(
    n_rows, n_attn, back, block,
    tok, gain_in, wq, wk, wv, docs_in, table, out,
    gain, docs, gains, xt, xn, wkv_buf, wq_buf, kbuf, vbuf, q, tops, acc, sums, qsum, tab, kdoc, qdoc, kmask,
    own_sem, w_send, w_recv, kv_send, kv_recv, ready,
):
    rows, width = tok.shape
    depth, kvw = wk.shape
    qw = wq.shape[1]
    kv_heads = kvw // HEAD
    group = qw // kvw
    tiles = rows // TQ
    mine = back * rows
    span = min(mine + rows, -(-(MOST - 1 + TQ) // TQ) * TQ)
    me = lax.axis_index("rows")
    at = lax.axis_index("attn")
    has_prev = at > 0
    has_next = at < n_attn - 1

    high = rows - block
    top = rows - TQ
    tok_parts = [(top + TQ // 2, TQ // 2, 2), (top, TQ // 2, 1)]
    tok_parts += [(c, TQ, 6 + i) for i, c in enumerate(reversed(range(high, top, TQ)))]
    tok_parts += [(0, high, 2)] if high else []

    def tok_copy(i):
        start, size, slot = tok_parts[i]
        here = pl.ds(start, size)
        return pltpu.make_async_copy(tok.at[here], xt.at[here], own_sem.at[slot])

    weights = [
        (wk, lambda d: wkv_buf.at[d, :, pl.ds(0, kvw)]),
        (wv, lambda d: wkv_buf.at[d, :, pl.ds(kvw, kvw)]),
        (wq, lambda d: wq_buf.at[d]),
    ]

    def own_copy(i):
        src, dst = weights[i]
        return pltpu.make_async_copy(src, dst(0), own_sem.at[(3, 0, 5)[i]])

    def weight_copy(d, i):
        src, dst = weights[i]
        return pltpu.make_async_remote_copy(
            src_ref=src, dst_ref=dst(d),
            send_sem=w_send.at[d - 1, i], recv_sem=w_recv.at[d - 1, i],
            device_id={"rows": lax.rem(me + d, n_rows)}, device_id_type=MESH,
        )

    small = [
        pltpu.make_async_copy(src, dst, own_sem.at[i])
        for i, (src, dst) in enumerate(((gain_in, gain), (docs_in, docs)))
    ]
    tab_copy = pltpu.make_async_copy(
        table.at[pl.ds(pl.multiple_of(at * rows, rows), rows)], tab, own_sem.at[4]
    )

    small[0].start()
    tok_copy(0).start()
    tok_copy(1).start()
    own_copy(0).start()
    near = range(2, 2 + (top - high) // TQ)
    for i in near:
        tok_copy(i).start()
    tab_copy.start()

    barrier = pltpu.get_barrier_semaphore()
    paired = n_rows == 2 and n_attn > 1
    if paired:
        first = me == 0

        @pl.when(jnp.logical_not(first))
        def _():
            pl.semaphore_signal(barrier, inc=1, device_id={"rows": 0}, device_id_type=MESH)

        @pl.when(first)
        def _():
            pl.semaphore_wait(barrier, 1)
            pl.semaphore_signal(ready, inc=1, device_id={"rows": 1}, device_id_type=MESH)

        @pl.when(jnp.logical_not(first))
        def _():
            pl.semaphore_wait(ready, 1)
    else:
        for d in range(1, n_rows):
            pl.semaphore_signal(
                barrier, inc=1, device_id={"rows": lax.rem(me + d, n_rows)}, device_id_type=MESH
            )
        if back:

            @pl.when(has_prev)
            def _():
                pl.semaphore_signal(
                    barrier, inc=1, device_id={"attn": at - 1}, device_id_type=MESH
                )

            pl.semaphore_wait(barrier, n_rows - 1 + has_next.astype(jnp.int32))
        elif n_rows > 1:
            pl.semaphore_wait(barrier, n_rows - 1)

    for i in range(2):
        for d in range(1, n_rows):
            weight_copy(d, i).start()
    if paired:

        @pl.when(has_prev)
        def _():
            pl.semaphore_signal(
                barrier, inc=1, device_id={"rows": 1, "attn": at - 1}, device_id_type=MESH
            )

    for s in range(back):

        @pl.when(at - back + s < 0)
        def _():
            kbuf[pl.ds(s * rows, rows), :] = jnp.zeros((rows, kvw), BF16)
            vbuf[pl.ds(s * rows, rows), :] = jnp.zeros((rows, kvw), BF16)

    copies = hop_copies(rows, block, back)

    def hop(p):
        s, _, which, start, size = copies[p]
        ref = (kbuf, vbuf)[which]
        return pltpu.make_async_remote_copy(
            src_ref=ref.at[pl.ds((back - s) * rows + start, size)],
            dst_ref=ref.at[pl.ds((back - s - 1) * rows + start, size)],
            send_sem=kv_send.at[s], recv_sem=kv_recv.at[p],
            device_id={"attn": jnp.minimum(at + 1, n_attn - 1)}, device_id_type=MESH,
        )

    def all_sent(s):
        ref = kbuf.at[pl.ds(0, 2 * rows)]
        pltpu.make_async_remote_copy(
            src_ref=ref, dst_ref=ref, send_sem=kv_send.at[s], recv_sem=kv_recv.at[0],
            device_id={"attn": jnp.minimum(at + 1, n_attn - 1)}, device_id_type=MESH,
        ).wait_send()

    def send(which, start, size):
        if back:

            @pl.when(has_next)
            def _():
                for p, (s, _, kind, row, _) in enumerate(copies):
                    if s == 0 and kind == which and start <= row < start + size:
                        hop(p).start()

    def arrived(wanted):
        if wanted:

            @pl.when(at > copies[wanted[0]][0])
            def _():
                for p in wanted:
                    hop(p).wait_recv()

    def relay(count):
        for _ in range(min(count, len(relays))):
            s, unit = relays.pop(0)
            arrived([p for p, c in enumerate(copies) if c[:2] == (s, unit)])

            @pl.when((at > s) & has_next)
            def _():
                for p, c in enumerate(copies):
                    if c[:2] == (s + 1, unit):
                        hop(p).start()

    relays = [(s, unit) for s in range(back - 1) for unit in range(2 * (rows // block))]

    strip, piece = 16, 256

    def norm(start, size):
        for first_row in reversed(range(start, start + size, 4 * strip)):
            norm_rows(first_row)

    def norm_rows(start):
        @pl.loop(0, 4, unroll=4)
        def _(i):
            here = pl.ds(pl.multiple_of(start + i * strip, strip), strip)
            squares = jnp.zeros((strip, piece), F32)
            for k in range(width // piece):
                x = xt[here, pl.ds(k * piece, piece)].astype(F32)
                squares = squares + x * x
            mean_sq = jnp.sum(squares, axis=-1, keepdims=True) * (1.0 / width)
            scale = jnp.broadcast_to(lax.rsqrt(mean_sq + 1e-05), (strip, piece))
            for k in range(width // piece):
                cols = pl.ds(k * piece, piece)
                x = xt[here, cols].astype(F32) * scale
                xn[here, cols] = (
                    x.reshape(strip // 8, 8, piece) * gains[:, cols][None]
                ).reshape(strip, piece).astype(BF16)

    lane = lax.broadcasted_iota(jnp.int32, (1, HEAD), 1)

    def tables(start, size):
        t = tab[pl.ds(start, size), :]
        swapped = pltpu.roll(t, HEAD // 2, 1)
        low = lane < HEAD // 2
        return jnp.where(low, t, swapped), jnp.where(low, -swapped, t)

    def rotate(u, cosine, sine):
        return (u * cosine + pltpu.roll(u, HEAD // 2, 1) * sine).astype(BF16)

    half = depth // 2 if depth % (2 * HEAD) == 0 else depth

    def dots(start, size, terms, weight):
        total = None
        for d, k in terms:
            owner = lax.rem(me - d + n_rows, n_rows)
            here = pl.ds(pl.multiple_of(owner * depth + k, half), half)
            term = jnp.dot(
                xn[pl.ds(start, size), here], weight(d, k), preferred_element_type=F32
            )
            total = term if total is None else total + term
        return total

    def project(start, size, first_col, cols):
        def weight(d, k):
            return wkv_buf[d, pl.ds(k, half), pl.ds(first_col, cols)]

        terms = [(d, k) for d in range(n_rows) for k in range(0, depth, half)]
        for chain in range(2):
            sums[chain, pl.ds(0, size), pl.ds(0, cols)] = dots(
                start, size, terms[chain::2], weight
            )
        return sums[0, pl.ds(0, size), pl.ds(0, cols)] + sums[1, pl.ds(0, size), pl.ds(0, cols)]

    def store_keys(start, size, total):
        cosine, sine = tables(start, size)
        for h in range(kv_heads):
            cols = pl.ds(h * HEAD, HEAD)
            kbuf[pl.ds(mine + start, size), cols] = rotate(
                total[:, h * HEAD : (h + 1) * HEAD], cosine, sine
            )

    def store_values(start, size, total):
        vbuf[pl.ds(mine + start, size), :] = total.astype(BF16)

    def weight_ready(i):
        for d in range(1, n_rows):
            weight_copy(d, i).wait_recv()

    tok_copy(0).wait()
    small[0].wait()
    gains[...] = jnp.broadcast_to(gain[...].astype(F32).reshape(1, -1), gains.shape)
    norm(top + TQ // 2, TQ // 2)
    tok_copy(1).wait()
    norm(top, TQ // 2)
    own_copy(1).start()
    if high:
        tok_copy(len(tok_parts) - 1).start()
    for d in range(1, n_rows):
        weight_copy(d, 2).start()
    small[1].start()
    own_copy(2).start()

    key_cols = pl.ds(0, kvw)

    def key_weight(d, k):
        return wkv_buf[d, pl.ds(k, half), key_cols]

    own = [(0, k) for k in range(0, depth, half)]
    far = [(d, k) for d in range(1, n_rows) for k in range(0, depth, half)]
    here = pl.ds(0, TQ)
    own_copy(0).wait()
    for i in near:
        tok_copy(i).wait()
    for chain in range(2):
        sums[chain, here, key_cols] = (
            dots(top, TQ, own[chain::2], key_weight)
            if own[chain::2]
            else jnp.zeros((TQ, kvw), F32)
        )
    for i in near:
        norm(tok_parts[i][0], TQ)
    tab_copy.wait()
    weight_ready(0)
    for chain in range(2):
        if far[chain::2]:
            sums[chain, here, key_cols] = sums[chain, here, key_cols] + dots(
                top, TQ, far[chain::2], key_weight
            )
    store_keys(top, TQ, sums[0, here, key_cols] + sums[1, here, key_cols])
    if paired:

        @pl.when(has_next & jnp.logical_not(first))
        def _():
            pl.semaphore_wait(barrier, 2)
            pl.semaphore_signal(ready, inc=1, device_id={"rows": 0}, device_id_type=MESH)

        @pl.when(has_next & first)
        def _():
            pl.semaphore_wait(ready, 1)

    send(0, top, TQ)
    for i in near:
        start = tok_parts[i][0]
        store_keys(start, TQ, project(start, TQ, 0, kvw))
        send(0, start, TQ)
    own_copy(1).wait()
    weight_ready(1)
    store_values(high, block, project(high, block, kvw, kvw))
    send(1, high, block)
    if high:
        tok_copy(len(tok_parts) - 1).wait()
        norm(0, high)
    for b in reversed(range(high // block)):
        store_keys(b * block, block, project(b * block, block, 0, kvw))
        send(0, b * block, block)
        store_values(b * block, block, project(b * block, block, kvw, kvw))
        send(1, b * block, block)
    small[1].wait()
    for s in range(back + 1):
        owner = at - back + s
        keep = pl.multiple_of(jnp.maximum(owner, 0) * rows, rows)
        kdoc[:, pl.ds(s * rows, rows)] = jnp.where(owner >= 0, docs[:, pl.ds(keep, rows)], -1)
    lanes = lax.broadcasted_iota(jnp.int32, (TQ, HEAD), 1)
    for k in range((back + 1) * tiles):
        here = pl.ds(k * TQ, TQ)
        column = jnp.broadcast_to(kdoc[:, here], (HEAD, TQ)).T
        same = column == lanes
        kmask[here, :] = jnp.where(same, 0.0, -1e30).astype(BF16)
        if k >= back * tiles:
            qdoc[pl.ds((k - back * tiles) * TQ, TQ), :] = column
            chosen = jnp.where(same, 1.0, 0.0).astype(BF16)
            for h in range(kv_heads):
                for g in range(group):
                    q[k - back * tiles, h, pl.ds(g * TQ, TQ), pl.ds(HEAD, HEAD)] = chosen

    def queries(start, d):
        owner = lax.rem(me - d + n_rows, n_rows)
        here = pl.ds(pl.multiple_of(owner * depth, depth), depth)
        return jnp.dot(xn[pl.ds(start, block), here], wq_buf[d], preferred_element_type=F32)

    steps = [b * block for b in reversed(range(rows // block))]
    own_copy(2).wait()
    for start in steps:
        qsum[pl.ds(start, block), :] = queries(start, 0)
    relay(1)
    for d in range(1, n_rows):
        weight_copy(d, 2).wait_recv()
    for start in steps:
        total = qsum[pl.ds(start, block), :]
        for d in range(1, n_rows):
            total = total + queries(start, d)
        cosine, sine = tables(start, block)
        for h in range(kv_heads):
            for g in range(group):
                col = (h * group + g) * HEAD
                u = rotate(total[:, col : col + HEAD], cosine, sine)
                for t in range(block // TQ):
                    q[start // TQ + t, h, pl.ds(g * TQ, TQ), pl.ds(0, HEAD)] = u[t * TQ : (t + 1) * TQ]
    relay(1)

    factor = math.log2(math.e) / math.sqrt(HEAD)

    def weigh(t, s, lo, size, opens):
        keys_at = pl.ds(s * rows + lo, size)
        made = []
        for h in range(kv_heads):
            keys = kbuf[keys_at, pl.ds(h * HEAD, HEAD)]
            small = s == 0 and size == TQ
            asked = q[t, h, :, pl.ds(0, HEAD)] if small else q[t, h]
            scores = lax.dot_general(
                asked,
                keys if small else jnp.concatenate([keys, kmask[keys_at, :]], axis=1),
                (((1,), (1,)), ((), ())),
                preferred_element_type=F32,
            )
            if small:
                seen = qdoc[pl.ds(t * TQ, TQ), :] == kdoc[:, keys_at]
                scores = jnp.where(
                    seen[None], scores.reshape(group, TQ, TQ), -1e30
                ).reshape(group * TQ, TQ)
            if s == back:
                ahead = lanes > lax.broadcasted_iota(jnp.int32, (TQ, HEAD), 0)
                edge = scores[:, size - TQ :].reshape(group, TQ, TQ)
                edge = jnp.where(ahead[None], -1e30, edge).reshape(group * TQ, TQ)
                scores = (
                    edge
                    if size == TQ
                    else jnp.concatenate([scores[:, : size - TQ], edge], axis=1)
                )
            top = jnp.broadcast_to(
                jnp.max(scores, axis=-1, keepdims=True), (group * TQ, HEAD)
            )
            fade = None
            if not opens:
                older = tops[t, h]
                top = jnp.maximum(older, top)
                fade = jnp.exp2((older - top) * factor)
            weight = jnp.exp2((scores - jnp.tile(top, (1, size // HEAD))) * factor).astype(BF16)
            made.append((weight, fade))
            tops[t, h] = top
        return made

    def mix(t, s, lo, size, made, closes):
        keys_at = pl.ds(s * rows + lo, size)
        for h in range(kv_heads):
            weight, fade = made[h]
            mixed = jnp.dot(
                weight,
                jnp.concatenate(
                    [vbuf[keys_at, pl.ds(h * HEAD, HEAD)], jnp.ones((size, HEAD), BF16)], axis=1
                ),
                preferred_element_type=F32,
            )
            if fade is not None:
                mixed = acc[t, h] * jnp.tile(fade, (1, 2)) + mixed
            if closes:
                done = (mixed[:, :HEAD] / mixed[:, HEAD:]).astype(BF16)
                for g in range(group):
                    out[pl.ds(t * TQ, TQ), pl.ds((h * group + g) * HEAD, HEAD)] = done[
                        g * TQ : (g + 1) * TQ
                    ]
            else:
                acc[t, h] = mixed

    def attend(t, s, lo, size, opens, closes):
        mix(t, s, lo, size, weigh(t, s, lo, size, opens), closes)

    def reach(t, s):
        return max(mine + (t + 1) * TQ - span - s * rows, 0)

    def final(t, s, lo):
        return lo <= reach(t, s) and all(reach(t, b) >= rows for b in range(s))

    for i, t in enumerate(reversed(range(tiles))):
        lo = reach(t, back)
        attend(t, back, lo, (t + 1) * TQ - lo, True, final(t, back, lo))
        if i % 2:
            relay(1)
    relay(len(relays))
    for s in reversed(range(1, back)):
        for t in reversed(range(tiles)):
            lo = reach(t, s)
            if lo < rows:
                attend(t, s, lo, rows - lo, False, final(t, s, lo))
    for i in range(len(weights)):
        for d in range(1, n_rows):
            weight_copy(d, i).wait_send()
    def come(which, start, size):
        arrived([
            p
            for p, (s, _, kind, row, length) in enumerate(copies)
            if s == back - 1 and kind == which and start < row + length <= start + size
        ])

    def sent_all():
        for s in range(back):

            @pl.when((at >= s) & has_next)
            def _():
                all_sent(s)

    blocks = list(reversed(range(0, rows, block))) if back else []
    for start in blocks:
        end = start + block
        low = {t: max(reach(t, 0), start) for t in reversed(range(tiles))}
        low = {t: lo for t, lo in low.items() if lo < end}
        if start == high and start > 0:
            come(0, start, block)
            made = {t: weigh(t, 0, lo, end - lo, False) for t, lo in low.items()}
            come(1, start, block)
            for t, lo in low.items():
                mix(t, 0, lo, end - lo, made[t], final(t, 0, lo))
            continue
        pairs = [(t, h) for t in low for h in range(kv_heads)]
        base = {(t, h): acc[t, h][:, :HEAD] for t, h in pairs}
        total = {(t, h): acc[t, h][:, HEAD:] for t, h in pairs}
        made = {}
        for c in reversed(range(start, end, TQ)):
            come(0, c, TQ)
            for t, lo in low.items():
                if lo > c:
                    continue
                for h, (weight, fade) in enumerate(weigh(t, 0, c, TQ, False)):
                    for e in range(c + TQ, end, TQ):
                        older, carry = made[t, h, e]
                        made[t, h, e] = older, fade if carry is None else carry * fade
                    made[t, h, c] = weight, None
                    base[t, h] = base[t, h] * fade
                    total[t, h] = total[t, h] * fade + jnp.dot(
                        weight, jnp.ones((TQ, HEAD), BF16), preferred_element_type=F32
                    )
                    if c == lo and final(t, 0, lo):
                        total[t, h] = 1.0 / total[t, h]
        for c in reversed(range(start, end, TQ)):
            if c == 0:
                sent_all()
            come(1, c, TQ)
            for t, h in pairs:
                if low[t] > c:
                    continue
                weight, carry = made[t, h, c]
                side = group * TQ // 2
                fresh = jnp.concatenate(
                    [
                        jnp.dot(
                            weight[e : e + side], vbuf[pl.ds(c, TQ), pl.ds(h * HEAD, HEAD)],
                            preferred_element_type=F32,
                        )
                        for e in (0, side)
                    ],
                    axis=0,
                )
                base[t, h] = base[t, h] + (fresh if carry is None else fresh * carry)
                if low[t] < c:
                    continue
                if final(t, 0, low[t]):
                    done = (base[t, h] * total[t, h]).astype(BF16)
                    for g in range(group):
                        out[pl.ds(t * TQ, TQ), pl.ds((h * group + g) * HEAD, HEAD)] = done[
                            g * TQ : (g + 1) * TQ
                        ]
                else:
                    acc[t, h] = jnp.concatenate([base[t, h], total[t, h]], axis=1)


def solution(mesh):
    n_rows = mesh.shape["rows"]
    n_attn = mesh.shape["attn"]

    def on_device(tokens, norm_gain, w_query, w_key, w_value, documents):
        rows, width = tokens.shape
        depth, qw = w_query.shape
        kvw = w_key.shape[1]
        back = min(n_attn - 1, -(-(MOST - 1) // rows))
        block = 2 * TQ if rows % (2 * TQ) == 0 else rows
        hops = len(hop_copies(rows, block, back))
        near = (block - TQ) // TQ
        table = jnp.asarray(rotary_table(documents.shape[1]))
        hbm = pl.BlockSpec(memory_space=pl.ANY)
        vmem = pl.BlockSpec(memory_space=pltpu.VMEM)
        keys = (back + 1) * rows
        group = qw // kvw
        heads = kvw // HEAD
        tiles = rows // TQ
        args = (tokens, norm_gain, w_query, w_key, w_value, documents, table)
        return pl.pallas_call(
            functools.partial(kernel, n_rows, n_attn, back, block),
            out_shape=pltpu.VMEM((rows, qw), BF16),
            in_specs=[hbm] * len(args),
            out_specs=vmem,
            scratch_shapes=[
                pltpu.VMEM((width,), BF16),
                pltpu.VMEM(documents.shape, jnp.int32),
                pltpu.VMEM((8, width), F32),
                pltpu.VMEM((rows, width), BF16),
                pltpu.VMEM((rows, width), BF16),
                pltpu.VMEM((n_rows, depth, 2 * kvw), BF16),
                pltpu.VMEM((n_rows, depth, qw), BF16),
                pltpu.VMEM((keys, kvw), BF16),
                pltpu.VMEM((keys, kvw), BF16),
                pltpu.VMEM((tiles, heads, group * TQ, 2 * HEAD), BF16),
                pltpu.VMEM((tiles, heads, group * TQ, HEAD), F32),
                pltpu.VMEM((tiles, heads, group * TQ, 2 * HEAD), F32),
                pltpu.VMEM((2, block, 2 * kvw), F32),
                pltpu.VMEM((rows, qw), F32),
                pltpu.VMEM((rows, HEAD), F32),
                pltpu.VMEM((1, keys), jnp.int32),
                pltpu.VMEM((rows, HEAD), jnp.int32),
                pltpu.VMEM((keys, HEAD), BF16),
                pltpu.SemaphoreType.DMA((6 + near,)),
                pltpu.SemaphoreType.DMA((max(n_rows - 1, 1), 3)),
                pltpu.SemaphoreType.DMA((max(n_rows - 1, 1), 3)),
                pltpu.SemaphoreType.DMA((max(back, 1),)),
                pltpu.SemaphoreType.DMA((max(hops, 1),)),
                pltpu.SemaphoreType.REGULAR,
            ],
            compiler_params=pltpu.CompilerParams(
                collective_id=0, has_side_effects=True, vmem_limit_bytes=48 << 20
            ),
            name="layer",
        )(*(pltpu.with_memory_space_constraint(a, pltpu.HBM) for a in args))

    placed = (
        P(("rows", "attn"), None),
        P(),
        P("rows", "tp"),
        P("rows", "tp"),
        P("rows", "tp"),
        P("rows", None),
    )
    return jax.shard_map(
        on_device, mesh=mesh, in_specs=placed, out_specs=P(("rows", "attn"), "tp"), check_vma=False
    )
```

```python
import functools
import math

import jax
import jax.numpy as jnp
import numpy as np
from jax import lax
from jax.experimental import pallas as pl
from jax.experimental.pallas import tpu as pltpu
from jax.sharding import PartitionSpec as P

HEAD = 128
MOST = 1024
TQ = 128
BF16 = jnp.bfloat16
F32 = jnp.float32
MESH = pl.DeviceIdType.MESH


def rotary_table(window):
    half = HEAD // 2
    frequency = np.exp(
        np.arange(half, dtype=np.float32) * np.float32(-2.0 * math.log(500000.0) / HEAD)
    ).astype(np.float32)
    angles = np.arange(window, dtype=np.float32)[:, None] * frequency[None, :]
    return np.concatenate([np.cos(angles), np.sin(angles)], axis=1).astype(np.float32)


def hop_copies(rows, block, back):
    copies = []
    for s in range(back):
        unit = 0
        for b in reversed(range(rows // block)):
            for which in range(2):
                upper = b == rows // block - 1
                fine = (upper and which == 0) if s == 0 else (s == back - 1 and not upper)
                size = TQ if fine else block
                for start in reversed(range(b * block, (b + 1) * block, size)):
                    copies.append((s, unit, which, start, size))
                unit += 1
    return copies


def kernel(
    n_rows, n_attn, back, block,
    tok, gain_in, wq, wk, wv, docs_in, table, out,
    gain, docs, gains, xt, xn, wkv_buf, wq_buf, kbuf, vbuf, q, tops, acc, sums, qsum, tab, kdoc, qdoc, kmask,
    own_sem, w_send, w_recv, kv_send, kv_recv, ready,
):
    rows, width = tok.shape
    depth, kvw = wk.shape
    qw = wq.shape[1]
    kv_heads = kvw // HEAD
    group = qw // kvw
    tiles = rows // TQ
    mine = back * rows
    span = min(mine + rows, -(-(MOST - 1 + TQ) // TQ) * TQ)
    me = lax.axis_index("rows")
    at = lax.axis_index("attn")
    has_prev = at > 0
    has_next = at < n_attn - 1

    high = rows - block
    top = rows - TQ
    tok_parts = [(top + TQ // 2, TQ // 2, 2), (top, TQ // 2, 1)]
    tok_parts += [(c, TQ, 6 + i) for i, c in enumerate(reversed(range(high, top, TQ)))]
    tok_parts += [(0, high, 2)] if high else []

    def tok_copy(i):
        start, size, slot = tok_parts[i]
        here = pl.ds(start, size)
        return pltpu.make_async_copy(tok.at[here], xt.at[here], own_sem.at[slot])

    weights = [
        (wk, lambda d: wkv_buf.at[d, :, pl.ds(0, kvw)]),
        (wv, lambda d: wkv_buf.at[d, :, pl.ds(kvw, kvw)]),
        (wq, lambda d: wq_buf.at[d]),
    ]

    def own_copy(i):
        src, dst = weights[i]
        return pltpu.make_async_copy(src, dst(0), own_sem.at[(3, 0, 5)[i]])

    def weight_copy(d, i):
        src, dst = weights[i]
        return pltpu.make_async_remote_copy(
            src_ref=src, dst_ref=dst(d),
            send_sem=w_send.at[d - 1, i], recv_sem=w_recv.at[d - 1, i],
            device_id={"rows": lax.rem(me + d, n_rows)}, device_id_type=MESH,
        )

    small = [
        pltpu.make_async_copy(src, dst, own_sem.at[i])
        for i, (src, dst) in enumerate(((gain_in, gain), (docs_in, docs)))
    ]
    tab_copy = pltpu.make_async_copy(
        table.at[pl.ds(pl.multiple_of(at * rows, rows), rows)], tab, own_sem.at[4]
    )

    small[0].start()
    tok_copy(0).start()
    tok_copy(1).start()
    near = range(2, 2 + (top - high) // TQ)
    for i in near:
        tok_copy(i).start()
    own_copy(0).start()
    tab_copy.start()

    barrier = pltpu.get_barrier_semaphore()
    paired = n_rows == 2 and n_attn > 1
    if paired:
        first = me == 0

        @pl.when(jnp.logical_not(first))
        def _():
            pl.semaphore_signal(barrier, inc=1, device_id={"rows": 0}, device_id_type=MESH)

        @pl.when(first)
        def _():
            pl.semaphore_wait(barrier, 1)
            pl.semaphore_signal(ready, inc=1, device_id={"rows": 1}, device_id_type=MESH)

        @pl.when(jnp.logical_not(first))
        def _():
            pl.semaphore_wait(ready, 1)
    else:
        for d in range(1, n_rows):
            pl.semaphore_signal(
                barrier, inc=1, device_id={"rows": lax.rem(me + d, n_rows)}, device_id_type=MESH
            )
        if back:

            @pl.when(has_prev)
            def _():
                pl.semaphore_signal(
                    barrier, inc=1, device_id={"attn": at - 1}, device_id_type=MESH
                )

            pl.semaphore_wait(barrier, n_rows - 1 + has_next.astype(jnp.int32))
        elif n_rows > 1:
            pl.semaphore_wait(barrier, n_rows - 1)

    for i in range(2):
        for d in range(1, n_rows):
            weight_copy(d, i).start()
    if paired:

        @pl.when(has_prev)
        def _():
            pl.semaphore_signal(
                barrier, inc=1, device_id={"rows": 1, "attn": at - 1}, device_id_type=MESH
            )

    for s in range(back):

        @pl.when(at - back + s < 0)
        def _():
            kbuf[pl.ds(s * rows, rows), :] = jnp.zeros((rows, kvw), BF16)
            vbuf[pl.ds(s * rows, rows), :] = jnp.zeros((rows, kvw), BF16)

    copies = hop_copies(rows, block, back)

    def hop(p):
        s, _, which, start, size = copies[p]
        ref = (kbuf, vbuf)[which]
        return pltpu.make_async_remote_copy(
            src_ref=ref.at[pl.ds((back - s) * rows + start, size)],
            dst_ref=ref.at[pl.ds((back - s - 1) * rows + start, size)],
            send_sem=kv_send.at[s], recv_sem=kv_recv.at[p],
            device_id={"attn": jnp.minimum(at + 1, n_attn - 1)}, device_id_type=MESH,
        )

    def all_sent(s):
        ref = kbuf.at[pl.ds(0, 2 * rows)]
        pltpu.make_async_remote_copy(
            src_ref=ref, dst_ref=ref, send_sem=kv_send.at[s], recv_sem=kv_recv.at[0],
            device_id={"attn": jnp.minimum(at + 1, n_attn - 1)}, device_id_type=MESH,
        ).wait_send()

    def send(which, start, size):
        if back:

            @pl.when(has_next)
            def _():
                for p, (s, _, kind, row, _) in enumerate(copies):
                    if s == 0 and kind == which and start <= row < start + size:
                        hop(p).start()

    def arrived(wanted):
        if wanted:

            @pl.when(at > copies[wanted[0]][0])
            def _():
                for p in wanted:
                    hop(p).wait_recv()

    def relay(count):
        for _ in range(min(count, len(relays))):
            s, unit = relays.pop(0)
            arrived([p for p, c in enumerate(copies) if c[:2] == (s, unit)])

            @pl.when((at > s) & has_next)
            def _():
                for p, c in enumerate(copies):
                    if c[:2] == (s + 1, unit):
                        hop(p).start()

    relays = [(s, unit) for s in range(back - 1) for unit in range(2 * (rows // block))]

    strip, piece = 16, 256

    def norm(start, size):
        for first_row in reversed(range(start, start + size, 4 * strip)):
            norm_rows(first_row)

    def norm_rows(start):
        @pl.loop(0, 4, unroll=4)
        def _(i):
            here = pl.ds(pl.multiple_of(start + i * strip, strip), strip)
            squares = jnp.zeros((strip, piece), F32)
            for k in range(width // piece):
                x = xt[here, pl.ds(k * piece, piece)].astype(F32)
                squares = squares + x * x
            mean_sq = jnp.sum(squares, axis=-1, keepdims=True) * (1.0 / width)
            scale = jnp.broadcast_to(lax.rsqrt(mean_sq + 1e-05), (strip, piece))
            for k in range(width // piece):
                cols = pl.ds(k * piece, piece)
                x = xt[here, cols].astype(F32) * scale
                xn[here, cols] = (
                    x.reshape(strip // 8, 8, piece) * gains[:, cols][None]
                ).reshape(strip, piece).astype(BF16)

    lane = lax.broadcasted_iota(jnp.int32, (1, HEAD), 1)

    def tables(start, size):
        t = tab[pl.ds(start, size), :]
        swapped = pltpu.roll(t, HEAD // 2, 1)
        low = lane < HEAD // 2
        return jnp.where(low, t, swapped), jnp.where(low, -swapped, t)

    def rotate(u, cosine, sine):
        return (u * cosine + pltpu.roll(u, HEAD // 2, 1) * sine).astype(BF16)

    half = depth // 2 if depth % (2 * HEAD) == 0 else depth

    def dots(start, size, terms, weight):
        total = None
        for d, k in terms:
            owner = lax.rem(me - d + n_rows, n_rows)
            here = pl.ds(pl.multiple_of(owner * depth + k, half), half)
            term = jnp.dot(
                xn[pl.ds(start, size), here], weight(d, k), preferred_element_type=F32
            )
            total = term if total is None else total + term
        return total

    def project(start, size, first_col, cols):
        def weight(d, k):
            return wkv_buf[d, pl.ds(k, half), pl.ds(first_col, cols)]

        terms = [(d, k) for d in range(n_rows) for k in range(0, depth, half)]
        for chain in range(2):
            sums[chain, pl.ds(0, size), pl.ds(0, cols)] = dots(
                start, size, terms[chain::2], weight
            )
        return sums[0, pl.ds(0, size), pl.ds(0, cols)] + sums[1, pl.ds(0, size), pl.ds(0, cols)]

    def store_keys(start, size, total):
        cosine, sine = tables(start, size)
        for h in range(kv_heads):
            cols = pl.ds(h * HEAD, HEAD)
            kbuf[pl.ds(mine + start, size), cols] = rotate(
                total[:, h * HEAD : (h + 1) * HEAD], cosine, sine
            )

    def store_values(start, size, total):
        vbuf[pl.ds(mine + start, size), :] = total.astype(BF16)

    def weight_ready(i):
        for d in range(1, n_rows):
            weight_copy(d, i).wait_recv()

    tok_copy(0).wait()
    small[0].wait()
    gains[...] = jnp.broadcast_to(gain[...].astype(F32).reshape(1, -1), gains.shape)
    norm(top + TQ // 2, TQ // 2)
    tok_copy(1).wait()
    norm(top, TQ // 2)
    own_copy(1).start()
    if high:
        tok_copy(len(tok_parts) - 1).start()
    for d in range(1, n_rows):
        weight_copy(d, 2).start()
    small[1].start()
    own_copy(2).start()

    key_cols = pl.ds(0, kvw)

    def key_weight(d, k):
        return wkv_buf[d, pl.ds(k, half), key_cols]

    own = [(0, k) for k in range(0, depth, half)]
    far = [(d, k) for d in range(1, n_rows) for k in range(0, depth, half)]
    here = pl.ds(0, TQ)
    for i in near:
        tok_copy(i).wait()
        norm(tok_parts[i][0] + TQ // 2, TQ // 2)
    own_copy(0).wait()
    for chain in range(2):
        sums[chain, here, key_cols] = (
            dots(top, TQ, own[chain::2], key_weight)
            if own[chain::2]
            else jnp.zeros((TQ, kvw), F32)
        )
    for i in near:
        norm(tok_parts[i][0], TQ // 2)
    tab_copy.wait()
    weight_ready(0)
    for chain in range(2):
        if far[chain::2]:
            sums[chain, here, key_cols] = sums[chain, here, key_cols] + dots(
                top, TQ, far[chain::2], key_weight
            )
    store_keys(top, TQ, sums[0, here, key_cols] + sums[1, here, key_cols])
    if paired:

        @pl.when(has_next & jnp.logical_not(first))
        def _():
            pl.semaphore_wait(barrier, 2)
            pl.semaphore_signal(ready, inc=1, device_id={"rows": 0}, device_id_type=MESH)

        @pl.when(has_next & first)
        def _():
            pl.semaphore_wait(ready, 1)

    send(0, top, TQ)
    for i in near:
        start = tok_parts[i][0]
        store_keys(start, TQ, project(start, TQ, 0, kvw))
        send(0, start, TQ)
    own_copy(1).wait()
    weight_ready(1)
    store_values(high, block, project(high, block, kvw, kvw))
    send(1, high, block)
    if high:
        tok_copy(len(tok_parts) - 1).wait()
        norm(0, high)
    for b in reversed(range(high // block)):
        store_keys(b * block, block, project(b * block, block, 0, kvw))
        send(0, b * block, block)
        store_values(b * block, block, project(b * block, block, kvw, kvw))
        send(1, b * block, block)
    small[1].wait()
    for s in range(back + 1):
        owner = at - back + s
        keep = pl.multiple_of(jnp.maximum(owner, 0) * rows, rows)
        kdoc[:, pl.ds(s * rows, rows)] = jnp.where(owner >= 0, docs[:, pl.ds(keep, rows)], -1)
    lanes = lax.broadcasted_iota(jnp.int32, (TQ, HEAD), 1)
    for k in range((back + 1) * tiles):
        here = pl.ds(k * TQ, TQ)
        column = jnp.broadcast_to(kdoc[:, here], (HEAD, TQ)).T
        same = column == lanes
        kmask[here, :] = jnp.where(same, 0.0, -1e30).astype(BF16)
        if k >= back * tiles:
            qdoc[pl.ds((k - back * tiles) * TQ, TQ), :] = column
            chosen = jnp.where(same, 1.0, 0.0).astype(BF16)
            for h in range(kv_heads):
                for g in range(group):
                    q[k - back * tiles, h, pl.ds(g * TQ, TQ), pl.ds(HEAD, HEAD)] = chosen

    def queries(start, d):
        owner = lax.rem(me - d + n_rows, n_rows)
        here = pl.ds(pl.multiple_of(owner * depth, depth), depth)
        return jnp.dot(xn[pl.ds(start, block), here], wq_buf[d], preferred_element_type=F32)

    steps = [b * block for b in reversed(range(rows // block))]
    own_copy(2).wait()
    for start in steps:
        qsum[pl.ds(start, block), :] = queries(start, 0)
    relay(1)
    for d in range(1, n_rows):
        weight_copy(d, 2).wait_recv()
    for start in steps:
        total = qsum[pl.ds(start, block), :]
        for d in range(1, n_rows):
            total = total + queries(start, d)
        cosine, sine = tables(start, block)
        for h in range(kv_heads):
            for g in range(group):
                col = (h * group + g) * HEAD
                u = rotate(total[:, col : col + HEAD], cosine, sine)
                for t in range(block // TQ):
                    q[start // TQ + t, h, pl.ds(g * TQ, TQ), pl.ds(0, HEAD)] = u[t * TQ : (t + 1) * TQ]
    relay(1)

    factor = math.log2(math.e) / math.sqrt(HEAD)

    def weigh(t, s, lo, size, opens):
        keys_at = pl.ds(s * rows + lo, size)
        made = []
        for h in range(kv_heads):
            keys = kbuf[keys_at, pl.ds(h * HEAD, HEAD)]
            small = s == 0 and size == TQ
            asked = q[t, h, :, pl.ds(0, HEAD)] if small else q[t, h]
            scores = lax.dot_general(
                asked,
                keys if small else jnp.concatenate([keys, kmask[keys_at, :]], axis=1),
                (((1,), (1,)), ((), ())),
                preferred_element_type=F32,
            )
            if small:
                seen = qdoc[pl.ds(t * TQ, TQ), :] == kdoc[:, keys_at]
                scores = jnp.where(
                    seen[None], scores.reshape(group, TQ, TQ), -1e30
                ).reshape(group * TQ, TQ)
            if s == back:
                ahead = lanes > lax.broadcasted_iota(jnp.int32, (TQ, HEAD), 0)
                edge = scores[:, size - TQ :].reshape(group, TQ, TQ)
                edge = jnp.where(ahead[None], -1e30, edge).reshape(group * TQ, TQ)
                scores = (
                    edge
                    if size == TQ
                    else jnp.concatenate([scores[:, : size - TQ], edge], axis=1)
                )
            top = jnp.broadcast_to(
                jnp.max(scores, axis=-1, keepdims=True), (group * TQ, HEAD)
            )
            fade = None
            if not opens:
                older = tops[t, h]
                top = jnp.maximum(older, top)
                fade = jnp.exp2((older - top) * factor)
            weight = jnp.exp2((scores - jnp.tile(top, (1, size // HEAD))) * factor).astype(BF16)
            made.append((weight, fade))
            tops[t, h] = top
        return made

    def mix(t, s, lo, size, made, closes):
        keys_at = pl.ds(s * rows + lo, size)
        for h in range(kv_heads):
            weight, fade = made[h]
            mixed = jnp.dot(
                weight,
                jnp.concatenate(
                    [vbuf[keys_at, pl.ds(h * HEAD, HEAD)], jnp.ones((size, HEAD), BF16)], axis=1
                ),
                preferred_element_type=F32,
            )
            if fade is not None:
                mixed = acc[t, h] * jnp.tile(fade, (1, 2)) + mixed
            if closes:
                done = (mixed[:, :HEAD] / mixed[:, HEAD:]).astype(BF16)
                for g in range(group):
                    out[pl.ds(t * TQ, TQ), pl.ds((h * group + g) * HEAD, HEAD)] = done[
                        g * TQ : (g + 1) * TQ
                    ]
            else:
                acc[t, h] = mixed

    def attend(t, s, lo, size, opens, closes):
        mix(t, s, lo, size, weigh(t, s, lo, size, opens), closes)

    def reach(t, s):
        return max(mine + (t + 1) * TQ - span - s * rows, 0)

    def final(t, s, lo):
        return lo <= reach(t, s) and all(reach(t, b) >= rows for b in range(s))

    for i, t in enumerate(reversed(range(tiles))):
        lo = reach(t, back)
        attend(t, back, lo, (t + 1) * TQ - lo, True, final(t, back, lo))
        if i % 2:
            relay(1)
    relay(len(relays))
    for s in reversed(range(1, back)):
        for t in reversed(range(tiles)):
            lo = reach(t, s)
            if lo < rows:
                attend(t, s, lo, rows - lo, False, final(t, s, lo))
    for i in range(len(weights)):
        for d in range(1, n_rows):
            weight_copy(d, i).wait_send()
    def come(which, start, size):
        arrived([
            p
            for p, (s, _, kind, row, length) in enumerate(copies)
            if s == back - 1 and kind == which and start < row + length <= start + size
        ])

    def sent_all():
        for s in range(back):

            @pl.when((at >= s) & has_next)
            def _():
                all_sent(s)

    blocks = list(reversed(range(0, rows, block))) if back else []
    for start in blocks:
        end = start + block
        low = {t: max(reach(t, 0), start) for t in reversed(range(tiles))}
        low = {t: lo for t, lo in low.items() if lo < end}
        if start == high and start > 0:
            come(0, start, block)
            made = {t: weigh(t, 0, lo, end - lo, False) for t, lo in low.items()}
            come(1, start, block)
            for t, lo in low.items():
                mix(t, 0, lo, end - lo, made[t], final(t, 0, lo))
            continue
        pairs = [(t, h) for t in low for h in range(kv_heads)]
        base = {(t, h): acc[t, h][:, :HEAD] for t, h in pairs}
        total = {(t, h): acc[t, h][:, HEAD:] for t, h in pairs}
        made = {}
        for c in reversed(range(start, end, TQ)):
            come(0, c, TQ)
            for t, lo in low.items():
                if lo > c:
                    continue
                for h, (weight, fade) in enumerate(weigh(t, 0, c, TQ, False)):
                    for e in range(c + TQ, end, TQ):
                        older, carry = made[t, h, e]
                        made[t, h, e] = older, fade if carry is None else carry * fade
                    made[t, h, c] = weight, None
                    base[t, h] = base[t, h] * fade
                    total[t, h] = total[t, h] * fade + jnp.dot(
                        weight, jnp.ones((TQ, HEAD), BF16), preferred_element_type=F32
                    )
                    if c == lo and final(t, 0, lo):
                        total[t, h] = 1.0 / total[t, h]
        for c in reversed(range(start, end, TQ)):
            if c == 0:
                sent_all()
            come(1, c, TQ)
            for t, h in pairs:
                if low[t] > c:
                    continue
                weight, carry = made[t, h, c]
                side = group * TQ // 2
                fresh = jnp.concatenate(
                    [
                        jnp.dot(
                            weight[e : e + side], vbuf[pl.ds(c, TQ), pl.ds(h * HEAD, HEAD)],
                            preferred_element_type=F32,
                        )
                        for e in (0, side)
                    ],
                    axis=0,
                )
                base[t, h] = base[t, h] + (fresh if carry is None else fresh * carry)
                if low[t] < c:
                    continue
                if final(t, 0, low[t]):
                    done = (base[t, h] * total[t, h]).astype(BF16)
                    for g in range(group):
                        out[pl.ds(t * TQ, TQ), pl.ds((h * group + g) * HEAD, HEAD)] = done[
                            g * TQ : (g + 1) * TQ
                        ]
                else:
                    acc[t, h] = jnp.concatenate([base[t, h], total[t, h]], axis=1)


def solution(mesh):
    n_rows = mesh.shape["rows"]
    n_attn = mesh.shape["attn"]

    def on_device(tokens, norm_gain, w_query, w_key, w_value, documents):
        rows, width = tokens.shape
        depth, qw = w_query.shape
        kvw = w_key.shape[1]
        back = min(n_attn - 1, -(-(MOST - 1) // rows))
        block = 2 * TQ if rows % (2 * TQ) == 0 else rows
        hops = len(hop_copies(rows, block, back))
        near = (block - TQ) // TQ
        table = jnp.asarray(rotary_table(documents.shape[1]))
        hbm = pl.BlockSpec(memory_space=pl.ANY)
        vmem = pl.BlockSpec(memory_space=pltpu.VMEM)
        keys = (back + 1) * rows
        group = qw // kvw
        heads = kvw // HEAD
        tiles = rows // TQ
        args = (tokens, norm_gain, w_query, w_key, w_value, documents, table)
        return pl.pallas_call(
            functools.partial(kernel, n_rows, n_attn, back, block),
            out_shape=pltpu.VMEM((rows, qw), BF16),
            in_specs=[hbm] * len(args),
            out_specs=vmem,
            scratch_shapes=[
                pltpu.VMEM((width,), BF16),
                pltpu.VMEM(documents.shape, jnp.int32),
                pltpu.VMEM((8, width), F32),
                pltpu.VMEM((rows, width), BF16),
                pltpu.VMEM((rows, width), BF16),
                pltpu.VMEM((n_rows, depth, 2 * kvw), BF16),
                pltpu.VMEM((n_rows, depth, qw), BF16),
                pltpu.VMEM((keys, kvw), BF16),
                pltpu.VMEM((keys, kvw), BF16),
                pltpu.VMEM((tiles, heads, group * TQ, 2 * HEAD), BF16),
                pltpu.VMEM((tiles, heads, group * TQ, HEAD), F32),
                pltpu.VMEM((tiles, heads, group * TQ, 2 * HEAD), F32),
                pltpu.VMEM((2, block, 2 * kvw), F32),
                pltpu.VMEM((rows, qw), F32),
                pltpu.VMEM((rows, HEAD), F32),
                pltpu.VMEM((1, keys), jnp.int32),
                pltpu.VMEM((rows, HEAD), jnp.int32),
                pltpu.VMEM((keys, HEAD), BF16),
                pltpu.SemaphoreType.DMA((6 + near,)),
                pltpu.SemaphoreType.DMA((max(n_rows - 1, 1), 3)),
                pltpu.SemaphoreType.DMA((max(n_rows - 1, 1), 3)),
                pltpu.SemaphoreType.DMA((max(back, 1),)),
                pltpu.SemaphoreType.DMA((max(hops, 1),)),
                pltpu.SemaphoreType.REGULAR,
            ],
            compiler_params=pltpu.CompilerParams(
                collective_id=0, has_side_effects=True, vmem_limit_bytes=48 << 20
            ),
            name="layer",
        )(*(pltpu.with_memory_space_constraint(a, pltpu.HBM) for a in args))

    placed = (
        P(("rows", "attn"), None),
        P(),
        P("rows", "tp"),
        P("rows", "tp"),
        P("rows", "tp"),
        P("rows", None),
    )
    return jax.shard_map(
        on_device, mesh=mesh, in_specs=placed, out_specs=P(("rows", "attn"), "tp"), check_vma=False
    )
```
